32 devices in a mesh: stack: 2 (over y), acq: 4 (over z), lines: 4 (over x, core).
Axes of the slice: x: 2, y: 2, z: 4, core: 2. Of those that a mesh axis runs over, the one named last changes fastest.
Arguments:
- returned_radar_signal_data: bfloat16 [8, 2, 512, 4096], P(('stack', 'acq'), None, 'lines'), parts along dimension 0, may hold values from -6 to 6
- slant_replica_filter_response: float32 [8, 2, 4096], P(('stack', 'acq')), parts along dimension 0, may hold values from -6 to 6
- along_track_sharpening_slope: float32 [8, 4096], P(('stack', 'acq'), 'lines'), parts along dimension 0, may hold values from 0.25 to 1
- motion_shift_centroid_hz: float32 [8, 4096], P(('stack', 'acq'), 'lines'), parts along dimension 0, may hold values from -0.2 to 0.2
- valid_along_track_rows: int32 [8], P(('stack', 'acq')), parts along dimension 0, may hold values from 256 to 512, as said below
- reference_index: int32 [2], P('stack'), parts along dimension 0, may hold values from 0 to 3
- patch_offsets: int32 [8, 2, 4, 32], P(('stack', 'acq'), None, None, 'lines'), parts along dimension 0, may hold values from -64 to 64
Outputs:
- correlation: float32 [8, 2, 256, 2048], P(('stack', 'acq'), None, None, 'lines'), parts along dimension 0
The draws below stay inside these ranges and needn't reach their ends.
There are 2 independent parts, one for each index of `stack`. The reference program is written for one: setup_inputs(seed, part) draws one part's arguments, and reference() takes and returns one part's arrays. A program takes and returns all parts, laid end to end along the dimension named above; each array names one. Nothing has to cross between parts.
Inputs may be any that keep to these rules, and one draw needn't show every extreme that they name: `valid_along_track_rows`: some acquisition has all 512 lines valid and some exactly half of them.
All inputs are finite; a program needn't handle non-finite values.
Results may differ from the reference program's by a relative error of at most 0.0053.
Values may be sent and summed in bfloat16 or wider, within the bound.
A program may use at most 64 MiB of HBM per device.

```python
import math
import jax
import jax.numpy as jnp
from jax import lax

NA = 512
NR = 4096
PATCH = 64
ACQ = 4


def draw_valid_along_track_rows(key, part):
    counts = jax.random.randint(jax.random.fold_in(key, 11), (ACQ,), NA // 2, NA + 1)
    order = jax.random.permutation(jax.random.fold_in(key, 12), ACQ)
    counts = jnp.where(order == 0, NA, counts)
    counts = jnp.where(order == 1, NA // 2, counts)
    return counts.astype(jnp.int32)


def set_ends(array, own_key, least, top_value):
    longest = array.shape.index(max(array.shape))
    spots = []
    for shift in (0, 1):
        where = [jax.random.randint(jax.random.fold_in(own_key, axis), (), 0, length) for axis, length in enumerate(array.shape)]
        where[longest] = (where[longest] + shift) % array.shape[longest]
        spots.append(tuple(where))
    return array.at[spots[0]].set(least).at[spots[1]].set(top_value)


def block_scale(own_key, extent, pieces, least, high):
    gain, own = 1.0, jax.random.fold_in(own_key, 6)
    for axis_at, shards_of in pieces:
        draws = jnp.exp(jax.random.uniform(jax.random.fold_in(own, axis_at), (shards_of,), jnp.float32, least / len(pieces), high / len(pieces)))
        gain = gain * jnp.repeat(draws, extent[axis_at] // shards_of).reshape([-1 if axis == axis_at else 1 for axis in range(len(extent))])
    return gain


def bell_draw(own_key, shape, deviation, reach, shards=(), kind=jnp.bfloat16):
    level = block_scale(own_key, shape, shards, -0.22, 0.18) if shards else 1.0
    result = jax.random.normal(own_key, shape, jnp.float32) * deviation * level
    return jnp.minimum(jnp.maximum(result, -reach), reach).astype(kind)


def setup_inputs(seed: int = 0, part: int = 0) -> dict:
    key_list = jax.random.split(jax.random.key(seed), 8)
    own_keys = jax.random.split(jax.random.fold_in(key_list[7], part), 8)
    returned_radar_signal_data = bell_draw(own_keys[0], (ACQ, 2, NA, NR), 0.7, 6.0, ((0, 4), (2, 4)))
    slant_replica_filter_response = bell_draw(own_keys[1], (ACQ, 2, NR), 0.7, 6.0, ((0, 4),), jnp.float32)
    along_track_sharpening_slope = jnp.clip(jnp.exp(math.log(1.0) - 1.3862944 * jax.random.uniform(own_keys[2], (ACQ, NR), jnp.float32) ** block_scale(own_keys[2], (ACQ, NR), ((0, 4), (1, 4)), -0.2, 0.2)), 0.25, 1.0)
    motion_shift_centroid_hz = jnp.clip(jax.random.uniform(own_keys[3], (ACQ, NR), jnp.float32, -0.2, 0.2) * block_scale(own_keys[3], (ACQ, NR), ((0, 4), (1, 4)), -0.4, 0.0), -0.2, 0.2)
    valid_along_track_rows = draw_valid_along_track_rows(jax.random.fold_in(jax.random.fold_in(key_list[7], part), 71), part)
    reference_index = jax.random.randint(own_keys[5], (1,), 0, ACQ).astype(jnp.int32)
    patch_offsets = set_ends(jax.random.randint(own_keys[6], (ACQ, 2, NA // (2 * PATCH), NR // (2 * PATCH)), -PATCH, PATCH + 1), jax.random.fold_in(own_keys[6], 1), -PATCH, PATCH).astype(jnp.int32)
    return {"returned_radar_signal_data": returned_radar_signal_data, "slant_replica_filter_response": slant_replica_filter_response, "along_track_sharpening_slope": along_track_sharpening_slope, "motion_shift_centroid_hz": motion_shift_centroid_hz, "valid_along_track_rows": valid_along_track_rows, "reference_index": reference_index, "patch_offsets": patch_offsets}


eps = 1e-06

def sharpen_one_pulse_group(vectorized_inputs):
    raw_one, filter_one, rate_one, centre_one, valid_one = vectorized_inputs
    line_index = jnp.arange(NA, dtype=jnp.int32)[:, None]
    keep_mask = (line_index < valid_one).astype(jnp.float32)
    echo = lax.complex(raw_one[0].astype(jnp.float32) * keep_mask, raw_one[1].astype(jnp.float32) * keep_mask)
    spectrum = jnp.fft.fft(echo, axis=1) * lax.complex(filter_one[0], filter_one[1])[None, :]
    compressed = jnp.fft.ifft(spectrum, axis=1)
    real_part = lax.optimization_barrier(jnp.real(compressed).astype(jnp.bfloat16)).astype(jnp.float32)
    imaginary = lax.optimization_barrier(jnp.imag(compressed).astype(jnp.bfloat16)).astype(jnp.float32)
    along = jnp.fft.fft(lax.complex(real_part, imaginary), axis=0)
    freq_index = jnp.arange(NA, dtype=jnp.int32)
    signed_freq = jnp.where(freq_index >= NA // 2, freq_index - NA, freq_index).astype(jnp.float32) / NA
    offset_freq = signed_freq[:, None] - centre_one[None, :]
    phase_angle = math.pi * NA / 4.0 * rate_one[None, :] * offset_freq * offset_freq
    along = along * lax.complex(jnp.cos(phase_angle), jnp.sin(phase_angle))
    focused = jnp.fft.ifft(along, axis=0)
    return jnp.stack([jnp.real(focused), jnp.imag(focused)]).astype(jnp.bfloat16)

def reference(returned_radar_signal_data, slant_replica_filter_response, along_track_sharpening_slope, motion_shift_centroid_hz, valid_along_track_rows, reference_index, patch_offsets):
    sharpened_acquisition_pictures = lax.map(sharpen_one_pulse_group, (returned_radar_signal_data, slant_replica_filter_response, along_track_sharpening_slope, motion_shift_centroid_hz, valid_along_track_rows))
    primary_image = sharpened_acquisition_pictures[reference_index[0]].astype(jnp.float32)
    row_blocks = NA // (2 * PATCH)
    col_blocks = NR // (2 * PATCH)
    half = PATCH // 2
    blocks = primary_image.reshape(2, row_blocks, 2 * PATCH, col_blocks, 2 * PATCH)
    blocks = blocks[:, :, half:half + PATCH, :, half:half + PATCH]
    blocks = blocks.transpose(1, 3, 0, 2, 4).reshape(row_blocks * col_blocks, 2, PATCH, PATCH)
    primary_stack = lax.complex(blocks[:, 0], blocks[:, 1])
    primary_power = lax.optimization_barrier(jnp.mean(blocks[:, 0] * blocks[:, 0] + blocks[:, 1] * blocks[:, 1], axis=(1, 2)))
    primary_spectrum = jnp.fft.fft2(primary_stack)
    block_row = lax.broadcasted_iota(jnp.int32, (row_blocks, col_blocks), 0)
    block_col = lax.broadcasted_iota(jnp.int32, (row_blocks, col_blocks), 1)

    def correlate(vectorized_inputs):
        image, offsets = vectorized_inputs
        padded = jnp.pad(image.astype(jnp.float32), ((0, 0), (half, half), (half, half)))
        row_start = (2 * PATCH * block_row + PATCH + offsets[0]).reshape(-1)
        col_start = (2 * PATCH * block_col + PATCH + offsets[1]).reshape(-1)

        def window(start_row, start_col):
            zero = jnp.zeros((), jnp.int32)
            return lax.dynamic_slice(padded, (zero, start_row, start_col), (2, PATCH, PATCH))
        second_stack = jax.vmap(window)(row_start, col_start)
        second_power = lax.optimization_barrier(jnp.mean(second_stack[:, 0] * second_stack[:, 0] + second_stack[:, 1] * second_stack[:, 1], axis=(1, 2)))
        second_spectrum = jnp.fft.fft2(lax.complex(second_stack[:, 0], second_stack[:, 1]))
        surface = jnp.fft.ifft2(primary_spectrum * jnp.conj(second_spectrum))
        scale = 1.0 / (PATCH * jnp.sqrt(primary_power + eps) * jnp.sqrt(second_power + eps))
        surface = surface * scale[:, None, None]
        stacked = jnp.stack([jnp.real(surface), jnp.imag(surface)]).astype(jnp.float32)
        stacked = stacked.reshape(2, row_blocks, col_blocks, PATCH, PATCH).transpose(0, 1, 3, 2, 4)
        return stacked.reshape(2, row_blocks * PATCH, col_blocks * PATCH)
    return lax.map(correlate, (sharpened_acquisition_pictures, patch_offsets))
```

```python
import functools
import math

import jax
import jax.numpy as jnp
import numpy as np
from jax import lax
from jax.experimental import pallas as pl
from jax.experimental.pallas import tpu as pltpu
from jax.sharding import PartitionSpec as P

PATCH = 64
LANES = 128
eps = 1e-06
bf16 = jnp.bfloat16
f32 = jnp.float32


def dft(size, sign):
    index = np.arange(size)
    angle = 2.0 * np.pi * (np.outer(index, index) % size) / size
    return np.cos(angle) + 1j * sign * np.sin(angle)


def right_form(matrix):
    return np.block([[matrix.real, matrix.imag], [-matrix.imag, matrix.real]])


def left_form(matrix):
    return np.block([[matrix.real, -matrix.imag], [matrix.imag, matrix.real]])


def halves(matrix):
    high = np.asarray(matrix, np.float32).astype(bf16)
    low = (np.asarray(matrix, np.float64) - high.astype(np.float64)).astype(bf16)
    return np.stack([high, low])


def split(value):
    high = value.astype(bf16)
    return high, (value - high.astype(f32)).astype(bf16)


def dot(a, b):
    return jnp.dot(a, b, preferred_element_type=f32)


def dot_nt(a, b):
    return lax.dot_general(a, b, (((1,), (1,)), ((), ())), preferred_element_type=f32)


def dot_tn(a, b):
    return lax.dot_general(a, b, (((0,), (0,)), ((), ())), preferred_element_type=f32)


def fft_list(values, sign):
    count = len(values)
    if count == 1:
        return values
    even = fft_list(values[0::2], sign)
    odd = fft_list(values[1::2], sign)
    out = [None] * count
    for k in range(count // 2):
        re, im = odd[k]
        if k == 0:
            pass
        elif 4 * k == count:
            re, im = (-im, re) if sign > 0 else (im, -re)
        elif 8 * k == count:
            r = math.sqrt(0.5)
            re, im = ((re - im) * r, (re + im) * r) if sign > 0 else ((re + im) * r, (im - re) * r)
        elif 8 * k == 3 * count:
            r = math.sqrt(0.5)
            re, im = ((re + im) * -r, (re - im) * r) if sign > 0 else ((im - re) * r, (re + im) * -r)
        else:
            c = math.cos(2 * math.pi * k / count)
            s = sign * math.sin(2 * math.pi * k / count)
            re, im = re * c - im * s, re * s + im * c
        out[k] = (even[k][0] + re, even[k][1] + im)
        out[k + count // 2] = (even[k][0] - re, even[k][1] - im)
    return out


def range_block(r0, block, first, valid, echo_ref, filt_ref, tw_ref, fwd_ref, inv_ref, out_ref, zh, zl):
    lead = echo_ref.shape[2] // LANES
    peers, pairs = out_ref.shape[0], out_ref.shape[1] // 2
    group = 16
    low = lax.broadcasted_iota(jnp.int32, (group, LANES), 1) < PATCH

    def put(row, count, re, im):
        zh[row : row + count, :LANES], zl[row : row + count, :LANES] = split(re)
        zh[row : row + count, LANES:], zl[row : row + count, LANES:] = split(im)

    def product(m_ref):
        h = zh[...]
        return dot(h, m_ref[0]) + dot(zl[...], m_ref[0]) + dot(h, m_ref[1])

    for g in range(block // group):
        at = pl.multiple_of(r0 + g * group, group)
        line = first + at + lax.broadcasted_iota(jnp.int32, (group, 1), 0)
        keep = (line < valid).astype(f32)
        values = [
            tuple(
                echo_ref[q, pl.ds(at, group), LANES * a : LANES * a + LANES].astype(f32) * keep
                for q in range(2)
            )
            for a in range(lead)
        ]
        for c, (re, im) in enumerate(fft_list(values, -1.0)):
            tr, ti = tw_ref[0, c : c + 1, :], tw_ref[1, c : c + 1, :]
            put(c * block + g * group, group, re * tr - im * ti, re * ti + im * tr)
    y = product(fwd_ref)
    for c in range(lead):
        part = y[c * block : c * block + block]
        re, im = part[:, :LANES], part[:, LANES:]
        hr, hi = filt_ref[0, c : c + 1, :], filt_ref[1, c : c + 1, :]
        put(c * block, block, re * hr - im * hi, re * hi + im * hr)
    y = product(inv_ref)
    for g in range(block // group):
        at = pl.multiple_of(r0 + g * group, group)
        values = []
        for c in range(lead):
            part = y[c * block + g * group : c * block + g * group + group]
            re, im = part[:, :LANES], part[:, LANES:]
            tr, ti = tw_ref[0, c : c + 1, :], tw_ref[1, c : c + 1, :]
            values.append((re * tr + im * ti, im * tr - re * ti))
        values = fft_list(values, 1.0)
        for t in range(lead // 2):
            for q in range(2):
                even, odd = values[2 * t][q], values[2 * t + 1][q]
                near = jnp.where(low, even, pltpu.roll(odd, PATCH, 1))
                far = jnp.where(low, pltpu.roll(even, PATCH, 1), odd)
                to, m = divmod(t, pairs)
                out_ref[to, m, q, pl.ds(at, group), :] = near.astype(bf16)
                out_ref[to, pairs + m, q, pl.ds(at, group), :] = far.astype(bf16)


def unit_polys():
    z = 0.125 - 0.125 * np.cos(np.pi * (np.arange(400) + 0.5) / 400)
    f = np.sqrt(z)
    cosine = np.polynomial.Polynomial.fit(z, np.cos(2 * np.pi * f), 7, domain=[0, 0.25]).convert()
    sine = np.polynomial.Polynomial.fit(z, np.sin(2 * np.pi * f) / f, 6, domain=[0, 0.25]).convert()
    return [float(v) for v in cosine.coef], [float(v) for v in sine.coef]


def cos_sin_turns(turns):
    cosine, sine = unit_polys()
    frac = turns - jnp.round(turns)
    z = frac * frac

    def horner(coef):
        value = jnp.full_like(z, coef[-1])
        for v in coef[-2::-1]:
            value = value * z + v
        return value

    return horner(cosine), horner(sine) * frac


def stacked(matrix):
    return np.concatenate(list(halves(matrix)), axis=-2)


def both_halves(m, value):
    count = m.shape[0] // 2
    y = dot(m, jnp.concatenate(split(value), axis=1))
    y = y[:count] + y[count:]
    return y[:, :LANES] + y[:, LANES:]


def azimuth_block(p, in_ref, par_ref, fwd_ref, inv_ref, out_ref):
    total = in_ref.shape[2]
    lead = total // LANES
    values = [
        tuple(in_ref[p, q, LANES * a : LANES * a + LANES, :].astype(f32) for q in range(2))
        for a in range(lead)
    ]
    values = fft_list(values, -1.0)
    sharp = par_ref[p, 0] * (total / 8.0)
    centre = par_ref[p, 1]
    back = []
    for c in range(lead):
        y = both_halves(fwd_ref[c], jnp.concatenate(values[c], axis=0))
        k = c + lead * lax.broadcasted_iota(jnp.int32, (LANES, 1), 0)
        u = jnp.where(k >= total // 2, k - total, k).astype(f32) * (1.0 / total)
        w = u - centre
        co, si = cos_sin_turns(sharp * w * w)
        re, im = y[:LANES], y[LANES:]
        y = both_halves(
            inv_ref[c], jnp.concatenate([re * co - im * si, re * si + im * co], axis=0)
        )
        back.append((y[:LANES], y[LANES:]))
    half = PATCH // 2
    for a, pair in enumerate(fft_list(back, 1.0)):
        for q in range(2):
            value = (pair[q] * (1.0 / total)).astype(bf16).astype(f32)
            out_ref[p, q, LANES * a + half : LANES * a + half + LANES, :] = value


def focus_body(
    names, sizes, valid_hbm, root_hbm, off_hbm, echo_hbm, filt_in, slope_ref, centre_ref,
    tw_ref, ph_ref, rf_ref, ri_ref, af_hbm, ai_hbm, fr_hbm, ir_hbm, fl_hbm, il_hbm, ones_hbm,
    out_ref, valid_ref, root_ref, off_ref, echo_ref, af_ref, ai_ref, fr_ref, ir_ref, fl_ref,
    il_ref, ones_ref, filt_ref, par_ref, edge, zh, zl, comp, turned, image,
    halo_out, halo_in, crop, pass_up, pass_down, from_up, from_down, stack, power, small_sem, echo_sem, const_sem, send_sem, recv_sem, edge_send, edge_recv,
    halo_send, halo_recv, up_send, up_recv, down_send, down_recv,
):
    here = {name: lax.axis_index(name) for name in names}
    me, peers = here["lines"], sizes["lines"]
    spot, stack_size = here["acq"], sizes["acq"]
    rows, length = echo_ref.shape[1:]
    lead = length // LANES
    pairs = turned.shape[0] // 2
    total = turned.shape[2]
    row_blocks = total // LANES
    half = PATCH // 2
    block = rows // echo_sem.shape[0]
    blocks = rows // block

    small = [
        pltpu.make_async_copy(src, dst, small_sem.at[n])
        for n, (src, dst) in enumerate(
            [(valid_hbm, valid_ref), (root_hbm, root_ref), (off_hbm, off_ref)]
        )
    ]
    consts = [
        pltpu.make_async_copy(src, dst, const_sem.at[n])
        for n, (src, dst) in enumerate([
            (af_hbm, af_ref), (ai_hbm, ai_ref), (fr_hbm, fr_ref), (ir_hbm, ir_ref),
            (fl_hbm, fl_ref), (il_hbm, il_ref), (ones_hbm, ones_ref),
        ])
    ]

    def load(b):
        at = pl.ds(pl.multiple_of(b * block, block), block)
        return pltpu.make_async_copy(
            echo_hbm.at[0, :, at, :], echo_ref.at[:, at, :], echo_sem.at[b]
        )

    small[0].start()
    for b in range(blocks):
        load(b).start()
    for copy in small[1:] + consts:
        copy.start()

    def device(axis, index):
        return tuple(index if name == axis else here[name] for name in names)

    def remote(src, dst, send, recv, axis, index):
        return pltpu.make_async_remote_copy(
            src_ref=src, dst_ref=dst, send_sem=send, recv_sem=recv,
            device_id=device(axis, index), device_id_type=pl.DeviceIdType.MESH,
        )

    barrier = pltpu.get_barrier_semaphore()
    targets = [("lines", (me + d) % peers) for d in range(1, peers)]
    targets += [("acq", (spot + d) % stack_size) for d in (1, stack_size - 1)]
    for axis, index in targets:
        pl.semaphore_signal(
            barrier, inc=1, device_id=device(axis, index), device_id_type=pl.DeviceIdType.MESH
        )

    per = LANES // lead
    parts = []
    for q in range(2):
        v = jnp.concatenate(
            [filt_in[0, q : q + 1, LANES * r : LANES * r + LANES] for r in range(lead)], axis=0
        ).T
        parts.append(
            jnp.concatenate([v[lead * m : lead * m + lead] for m in range(per)], axis=1)
        )
    filt_ref[0] = parts[0] * ph_ref[0] - parts[1] * ph_ref[1]
    filt_ref[1] = parts[0] * ph_ref[1] + parts[1] * ph_ref[0]

    right, left_of = (me + 1) % peers, (me + peers - 1) % peers
    edges = [
        remote(
            ref.at[:, pl.ds(0, LANES)], edge.at[n], edge_send.at[n], edge_recv.at[n],
            "lines", left_of,
        )
        for n, ref in enumerate((slope_ref, centre_ref))
    ]

    def exchange(d, b, p):
        to = (me + d) % peers
        at = pl.ds(pl.multiple_of(b * block, block), block)
        land = pl.ds(pl.multiple_of(me * rows + b * block, block), block)
        return remote(
            comp.at[to, p, :, at, :], turned.at[p, :, land, :],
            send_sem.at[d - 1, b, p], recv_sem.at[d - 1, b, p], "lines", to,
        )

    order = sorted(range(1, peers), key=lambda d: -min(d, peers - d))

    def send(b, p):
        for d in order:
            exchange(d, b, p).start()

    small[0].wait()

    def compress(b, carry):
        r0 = pl.multiple_of(b * block, block)
        load(b).wait()
        range_block(
            r0, block, me * rows, valid_ref[0], echo_ref, filt_ref, tw_ref, rf_ref, ri_ref,
            comp, zh, zl,
        )
        turned[:, :, pl.ds(pl.multiple_of(me * rows + r0, block), block), :] = comp[
            me, :, :, pl.ds(r0, block), :
        ]

        @pl.when(b == 0)
        def _():
            pl.semaphore_wait(barrier, len(targets))

        lax.fori_loop(0, pairs, lambda p, x: (send(b, p), x)[1], 0)
        return carry

    lax.fori_loop(0, blocks, compress, 0)
    for copy in edges:
        copy.start()

    image[:, :, :half, :] = jnp.zeros((2 * pairs + 1, 2, half, LANES), f32)
    image[:, :, half + total :, :] = jnp.zeros((2 * pairs + 1, 2, half, LANES), f32)

    @pl.when(spot == 0)
    def _():
        from_up[...] = jnp.zeros_like(from_up)

    @pl.when(spot == stack_size - 1)
    def _():
        from_down[...] = jnp.zeros_like(from_down)

    for copy in small[1:] + consts:
        copy.wait()
    for copy in edges:
        copy.wait_recv()
    lane = lax.broadcasted_iota(jnp.int32, (1, LANES), 1)
    for n, ref in enumerate((slope_ref, centre_ref)):
        row = [
            pltpu.roll(ref[:, LANES * a : LANES * a + LANES], LANES - half, 1)
            for a in range(2 * pairs)
        ]
        row.append(pltpu.roll(edge[n], LANES - half, 1))
        row = [jnp.where(lane < LANES - half, row[a], row[a + 1]) for a in range(2 * pairs)]
        for m in range(pairs):
            even, odd = row[2 * m], row[2 * m + 1]
            par_ref[m, n] = jnp.where(lane < PATCH, even, pltpu.roll(odd, PATCH, 1))
            par_ref[pairs + m, n] = jnp.where(lane < PATCH, pltpu.roll(even, PATCH, 1), odd)

    mine = root_ref[0] == spot
    lanes = (
        (spot, from_up, pass_up, up_send, up_recv, 1),
        (stack_size - 1 - spot, from_down, pass_down, down_send, down_recv, -1),
    )

    def chain(at, src, buffer, sends, recvs, step):
        return remote(
            src.at[at], buffer.at[at], sends.at[at], recvs.at[at], "acq",
            (spot + step + stack_size) % stack_size,
        )

    def slot(s, carry):
        for depth, buffer, staged, sends, recvs, step in lanes:
            at = s - row_blocks * (depth - 1)

            @pl.when(jnp.logical_and(depth > 0, jnp.logical_and(at >= 0, at < pairs * row_blocks)))
            def _():
                copy = chain(at, staged, buffer, sends, recvs, step)
                copy.wait_recv()

                @pl.when(depth < stack_size - 1)
                def _():
                    staged[at] = jnp.where(mine, crop[at], buffer[at])
                    copy.start()

        return carry

    def receive(p):
        for d in order:
            for b in range(blocks):
                exchange(d, b, p).wait_recv()

    wide_lane = lax.broadcasted_iota(jnp.int32, (LANES, LANES), 1)
    low = wide_lane < PATCH
    halo = remote(halo_out, halo_in, halo_send.at[0], halo_recv.at[0], "lines", right)

    def near(m):
        def start(a, carry):
            at = m * row_blocks + a
            line = pl.ds(pl.multiple_of(a * LANES + PATCH, PATCH), PATCH)
            for q in range(2):
                crop[at, q] = image[m, q, line, :].astype(bf16)
            for depth, buffer, staged, sends, recvs, step in lanes:
                @pl.when(jnp.logical_and(depth == 0, stack_size > 1))
                def _():
                    chain(at, crop, buffer, sends, recvs, step).start()
            return carry

        lax.fori_loop(0, row_blocks, start, 0)

    def far():
        p = 2 * pairs - 1
        for q in range(2):
            for a in range(row_blocks // 2):
                at = slice(LANES * a, LANES * a + LANES)
                above = slice(LANES * a + half, LANES * a + half + LANES)
                below = slice(above.start + total // 2, above.stop + total // 2)
                halo_out[q, at, :] = jnp.where(
                    low, pltpu.roll(image[p, q, above, :], PATCH, 1), image[p, q, below, :]
                ).astype(bf16)
        halo.start()

        @pl.when(me == peers - 1)
        def _():
            for q in range(2):
                for a in range(row_blocks):
                    at = slice(LANES * a + half, LANES * a + half + LANES)
                    image[p, q, at, :] = jnp.where(
                        wide_lane < LANES - half, image[p, q, at, :], 0.0
                    )

    def take_halo():
        halo.wait_recv()
        outside = jnp.logical_and(wide_lane < LANES - half, me == 0)
        for q in range(2):
            for a in range(row_blocks // 2):
                value = halo_in[q, LANES * a : LANES * a + LANES, :].astype(f32)
                to = half + LANES * a
                image[2 * pairs, q, to : to + LANES, :] = jnp.where(
                    outside, 0.0, pltpu.roll(value, PATCH, 1)
                )
                to += total // 2
                image[2 * pairs, q, to : to + LANES, :] = jnp.where(outside, 0.0, value)

    patch_lane = lax.broadcasted_iota(jnp.int32, (PATCH, LANES), 1)

    def put(i, kind, pair):
        at = pl.ds(pl.multiple_of(PATCH * (kind * row_blocks + i), PATCH), PATCH)
        for q in range(2):
            stack[at, LANES * q : LANES * q + LANES] = pair[q].astype(bf16)
        re, im = pair
        power[pl.ds(kind * row_blocks + i, 1), :] = jnp.sum(re * re + im * im, axis=0, keepdims=True)

    def window(m, i):
        picked = []
        for s in range(2):
            across = off_ref[0, 1, i, 2 * m + s]
            down = pl.ds(LANES * i + PATCH + off_ref[0, 0, i, 2 * m + s], PATCH)
            back = across < 0
            turn = across + jnp.where(back, PATCH, 0)
            before = pairs + m if s else jnp.where(m == 0, 2 * pairs, pairs + m - 1)
            first = jnp.where(back, before, m)
            second = jnp.where(back, m, pairs + m)
            base = jnp.where(back, PATCH * (1 - s), PATCH * s)
            start = patch_lane - PATCH * s < PATCH - turn
            picked.append([
                jnp.where(
                    start,
                    pltpu.roll(
                        image[first, q, down, :], (2 * LANES + PATCH * s - base - turn) % LANES, 1
                    ),
                    pltpu.roll(image[second, q, down, :], (PATCH + LANES - turn) % LANES, 1),
                )
                for q in range(2)
            ])
        return [jnp.where(patch_lane < PATCH, picked[0][q], picked[1][q]) for q in range(2)]

    def left(m_ref, value):
        y = dot(m_ref[...], value.astype(bf16))
        return y[:LANES] + y[LANES:]

    def right_product(value, m_ref):
        return dot(value, m_ref[0]) + dot(value, m_ref[1])

    def correlate(m):
        def one(i, carry):
            put(i, 1, window(m, i))
            at = m * row_blocks + i
            put(i, 0, [
                jnp.where(
                    mine, crop[at, q],
                    jnp.where(root_ref[0] < spot, from_up[at, q], from_down[at, q]),
                ).astype(f32)
                for q in range(2)
            ])
            return carry

        lax.fori_loop(0, row_blocks, one, 0)
        y = right_product(stack[...], fr_ref)
        z = left(fl_ref, jnp.concatenate([
            jnp.concatenate(
                [
                    y[PATCH * n : PATCH * n + PATCH, LANES * q : LANES * q + LANES]
                    for n in range(2 * row_blocks)
                ],
                axis=1,
            )
            for q in range(2)
        ], axis=0))
        z, zs = z[:, : LANES * row_blocks], z[:, LANES * row_blocks :]
        pr, pi, sr, si = z[:PATCH], z[PATCH:], zs[:PATCH], zs[PATCH:]
        x = left(il_ref, jnp.concatenate([pr * sr + pi * si, pi * sr - pr * si], axis=0))
        x = jnp.concatenate([
            jnp.concatenate(
                [
                    x[PATCH * q : PATCH * q + PATCH, LANES * n : LANES * n + LANES]
                    for n in range(row_blocks)
                ],
                axis=0,
            )
            for q in range(2)
        ], axis=1)
        y = right_product(x.astype(bf16), ir_ref)
        means = jnp.dot(
            power[...], ones_ref[...], precision=lax.Precision.HIGHEST, preferred_element_type=f32
        )
        scale = lax.rsqrt(means + eps)
        factor = scale[:row_blocks] * scale[row_blocks:] * (1.0 / PATCH**3)
        to = pl.ds(pl.multiple_of(m * LANES, LANES), LANES)
        for i in range(row_blocks):
            for q in range(2):
                out_ref[0, q, PATCH * i : PATCH * i + PATCH, to] = (
                    y[PATCH * i : PATCH * i + PATCH, LANES * q : LANES * q + LANES]
                    * factor[i : i + 1, :]
                )

    ahead = row_blocks * max(stack_size - 4, 0)

    def step(t, carry):
        @pl.when(t == pairs - 1)
        def _():
            lax.fori_loop(0, row_blocks + ahead, slot, 0)

        @pl.when(t >= pairs)
        def _():
            s = ahead + row_blocks * (t - pairs + 1)
            lax.fori_loop(s, s + row_blocks, slot, 0)

        @pl.when(t < 2 * pairs)
        def _():
            p = t + (t // pairs) * ((t + pairs - 1) % pairs - t + pairs)
            receive(p)

            @pl.when(t < pairs)
            def _():
                nxt = pairs + (t + pairs - 1) % pairs
                lax.fori_loop(0, blocks, lambda b, x: (send(b, nxt), x)[1], 0)

            azimuth_block(p, turned, par_ref, af_ref, ai_ref, image)

            @pl.when(t < pairs)
            def _():
                near(t)

            @pl.when(t == pairs)
            def _():
                far()

        @pl.when(t > pairs)
        def _():
            @pl.when(t == pairs + 1)
            def _():
                take_halo()

            correlate(t - pairs - 1)

        return carry

    lax.fori_loop(0, 2 * pairs + 1, step, 0)

    for depth, buffer, staged, sends, recvs, step_by in lanes:

        @pl.when(depth < stack_size - 1)
        def _():
            lax.fori_loop(
                0, pairs * row_blocks,
                lambda n, x: (chain(n, staged, buffer, sends, recvs, step_by).wait_send(), x)[1], 0,
            )

    halo.wait_send()
    for copy in edges:
        copy.wait_send()

    def finish(p, carry):
        for d in order:
            for b in range(blocks):
                exchange(d, b, p).wait_send()
        return carry

    lax.fori_loop(0, 2 * pairs, finish, 0)


def focus(names, sizes, valid, root, echo, filt, slope, centre, offsets):
    rows, length = echo.shape[2:]
    lead = length // LANES
    block = min(rows, 32)
    blocks = rows // block
    total, cols = rows * sizes["lines"], slope.shape[1]
    peers = sizes["lines"]
    wide = 2 * LANES
    pairs = cols // wide
    row_blocks = total // LANES
    half = PATCH // 2
    place = np.arange(LANES)
    per = LANES // lead
    freq = per * (place % lead) + place // lead
    rf = halves(right_form(dft(LANES, -1.0)[:, freq]))
    ri = halves(right_form(dft(LANES, 1.0)[freq, :]))
    angle = 2 * np.pi * np.outer(np.arange(lead), place) / length
    tw = np.stack([np.cos(angle), -np.sin(angle)]).astype(np.float32)
    whole = np.arange(lead)[:, None] + lead * freq[None, :]
    angle = 2 * np.pi * ((half * whole) % length) / length
    ph = (np.stack([np.cos(angle), np.sin(angle)]) / length).astype(np.float32)
    fwd, inv = [], []
    for c in range(row_blocks):
        phase = np.exp(-2j * np.pi * c * place / total)
        matrix = dft(LANES, -1.0) * phase[None, :]
        fwd.append(left_form(matrix))
        inv.append(left_form(matrix.conj().T))
    fwd, inv = stacked(np.stack(fwd)), stacked(np.stack(inv))
    two = np.eye(2)
    fr = halves(right_form(np.kron(two, dft(PATCH, -1.0))))
    ir = halves(right_form(np.kron(two, dft(PATCH, 1.0))))
    fl = stacked(left_form(dft(PATCH, -1.0)))
    il = stacked(left_form(dft(PATCH, 1.0)))
    ones = np.kron(two, np.full((PATCH, PATCH), 1.0 / PATCH**2)).astype(np.float32)
    hbm, vmem = pl.BlockSpec(memory_space=pl.ANY), pl.BlockSpec(memory_space=pltpu.VMEM)
    dma = pltpu.SemaphoreType.DMA
    chunk = pltpu.VMEM((pairs * row_blocks, 2, PATCH, LANES), bf16)
    consts = (fwd, inv, fr, ir, fl, il, ones)
    return pl.pallas_call(
        functools.partial(focus_body, names, sizes),
        in_specs=[hbm] * 4 + [vmem] * 7 + [hbm] * 7,
        out_specs=vmem,
        out_shape=jax.ShapeDtypeStruct((1, 2, total // 2, cols // 2), f32),
        scratch_shapes=[
            pltpu.SMEM(valid.shape, jnp.int32),
            pltpu.SMEM(root.shape, jnp.int32),
            pltpu.SMEM(offsets.shape, jnp.int32),
            pltpu.VMEM((2, rows, length), bf16),
        ]
        + [pltpu.VMEM(c.shape, c.dtype) for c in consts]
        + [
            pltpu.VMEM((2, lead, LANES), f32),
            pltpu.VMEM((2 * pairs, 2, 1, LANES), f32),
            pltpu.VMEM((2, 1, LANES), f32),
            pltpu.VMEM((lead * block, wide), bf16),
            pltpu.VMEM((lead * block, wide), bf16),
            pltpu.VMEM((peers, 2 * pairs, 2, rows, LANES), bf16),
            pltpu.VMEM((2 * pairs, 2, total, LANES), bf16),
            pltpu.VMEM((2 * pairs + 1, 2, total + PATCH, LANES), f32),
            pltpu.VMEM((2, total // 2, LANES), bf16),
            pltpu.VMEM((2, total // 2, LANES), bf16),
        ]
        + [chunk] * 5
        + [
            pltpu.VMEM((2 * row_blocks * PATCH, wide), bf16),
            pltpu.VMEM((2 * row_blocks, LANES), f32),
        ]
        + [dma((3,)), dma((blocks,)), dma((len(consts),))]
        + [dma((peers - 1, blocks, 2 * pairs))] * 2
        + [dma((2,))] * 2
        + [dma((1,))] * 2
        + [dma((pairs * row_blocks,))] * 4,
        compiler_params=pltpu.CompilerParams(
            collective_id=0, has_side_effects=True, vmem_limit_bytes=63 * 1024 * 1024
        ),
        name="focus",
    )(valid, root, offsets, echo, filt, slope, centre, tw, ph, rf, ri, *consts)


def on_device(names, sizes, echo, filt, slope, centre, valid, reference_index, offsets):
    return focus(names, sizes, valid, reference_index, echo, filt, slope, centre, offsets)


def solution(mesh):
    names = tuple(mesh.axis_names)
    sizes = {name: int(mesh.shape[name]) for name in names}
    return jax.shard_map(
        functools.partial(on_device, names, sizes),
        mesh=mesh,
        in_specs=(
            P(("stack", "acq"), None, "lines", None),
            P(("stack", "acq"), None, None),
            P(("stack", "acq"), "lines"),
            P(("stack", "acq"), "lines"),
            P(("stack", "acq")),
            P("stack"),
            P(("stack", "acq"), None, None, "lines"),
        ),
        out_specs=P(("stack", "acq"), None, None, "lines"),
        check_vma=False,
    )
```

```python
import functools
import math

import jax
import jax.numpy as jnp
import numpy as np
from jax import lax
from jax.experimental import pallas as pl
from jax.experimental.pallas import tpu as pltpu
from jax.sharding import PartitionSpec as P

PATCH = 64
LANES = 128
eps = 1e-06
bf16 = jnp.bfloat16
f32 = jnp.float32


def dft(size, sign):
    index = np.arange(size)
    angle = 2.0 * np.pi * (np.outer(index, index) % size) / size
    return np.cos(angle) + 1j * sign * np.sin(angle)


def right_form(matrix):
    return np.block([[matrix.real, matrix.imag], [-matrix.imag, matrix.real]])


def left_form(matrix):
    return np.block([[matrix.real, -matrix.imag], [matrix.imag, matrix.real]])


def halves(matrix):
    high = np.asarray(matrix, np.float32).astype(bf16)
    low = (np.asarray(matrix, np.float64) - high.astype(np.float64)).astype(bf16)
    return np.stack([high, low])


def split(value):
    high = value.astype(bf16)
    return high, (value - high.astype(f32)).astype(bf16)


def dot(a, b):
    return jnp.dot(a, b, preferred_element_type=f32)


def dot_nt(a, b):
    return lax.dot_general(a, b, (((1,), (1,)), ((), ())), preferred_element_type=f32)


def dot_tn(a, b):
    return lax.dot_general(a, b, (((0,), (0,)), ((), ())), preferred_element_type=f32)


def fft_list(values, sign):
    count = len(values)
    if count == 1:
        return values
    even = fft_list(values[0::2], sign)
    odd = fft_list(values[1::2], sign)
    out = [None] * count
    for k in range(count // 2):
        re, im = odd[k]
        if k == 0:
            pass
        elif 4 * k == count:
            re, im = (-im, re) if sign > 0 else (im, -re)
        elif 8 * k == count:
            r = math.sqrt(0.5)
            re, im = ((re - im) * r, (re + im) * r) if sign > 0 else ((re + im) * r, (im - re) * r)
        elif 8 * k == 3 * count:
            r = math.sqrt(0.5)
            re, im = ((re + im) * -r, (re - im) * r) if sign > 0 else ((im - re) * r, (re + im) * -r)
        else:
            c = math.cos(2 * math.pi * k / count)
            s = sign * math.sin(2 * math.pi * k / count)
            re, im = re * c - im * s, re * s + im * c
        out[k] = (even[k][0] + re, even[k][1] + im)
        out[k + count // 2] = (even[k][0] - re, even[k][1] - im)
    return out


def range_block(r0, block, first, valid, echo_ref, filt_ref, tw_ref, fwd_ref, inv_ref, out_ref, zh, zl):
    lead = echo_ref.shape[2] // LANES
    peers, pairs = out_ref.shape[0], out_ref.shape[1] // 2
    group = 16
    low = lax.broadcasted_iota(jnp.int32, (group, LANES), 1) < PATCH

    def put(row, count, re, im):
        zh[row : row + count, :LANES], zl[row : row + count, :LANES] = split(re)
        zh[row : row + count, LANES:], zl[row : row + count, LANES:] = split(im)

    def product(m_ref):
        h = zh[...]
        return dot(h, m_ref[0]) + dot(zl[...], m_ref[0]) + dot(h, m_ref[1])

    for g in range(block // group):
        at = pl.multiple_of(r0 + g * group, group)
        line = first + at + lax.broadcasted_iota(jnp.int32, (group, 1), 0)
        keep = (line < valid).astype(f32)
        values = [
            tuple(
                echo_ref[q, pl.ds(at, group), LANES * a : LANES * a + LANES].astype(f32) * keep
                for q in range(2)
            )
            for a in range(lead)
        ]
        for c, (re, im) in enumerate(fft_list(values, -1.0)):
            tr, ti = tw_ref[0, c : c + 1, :], tw_ref[1, c : c + 1, :]
            put(c * block + g * group, group, re * tr - im * ti, re * ti + im * tr)
    y = product(fwd_ref)
    for c in range(lead):
        part = y[c * block : c * block + block]
        re, im = part[:, :LANES], part[:, LANES:]
        hr, hi = filt_ref[0, c : c + 1, :], filt_ref[1, c : c + 1, :]
        put(c * block, block, re * hr - im * hi, re * hi + im * hr)
    y = product(inv_ref)
    for g in range(block // group):
        at = pl.multiple_of(r0 + g * group, group)
        values = []
        for c in range(lead):
            part = y[c * block + g * group : c * block + g * group + group]
            re, im = part[:, :LANES], part[:, LANES:]
            tr, ti = tw_ref[0, c : c + 1, :], tw_ref[1, c : c + 1, :]
            values.append((re * tr + im * ti, im * tr - re * ti))
        values = fft_list(values, 1.0)
        for t in range(lead // 2):
            for q in range(2):
                even, odd = values[2 * t][q], values[2 * t + 1][q]
                near = jnp.where(low, even, pltpu.roll(odd, PATCH, 1))
                far = jnp.where(low, pltpu.roll(even, PATCH, 1), odd)
                to, m = divmod(t, pairs)
                out_ref[to, m, q, pl.ds(at, group), :] = near.astype(bf16)
                out_ref[to, pairs + m, q, pl.ds(at, group), :] = far.astype(bf16)


def unit_polys():
    z = 0.125 - 0.125 * np.cos(np.pi * (np.arange(400) + 0.5) / 400)
    f = np.sqrt(z)
    cosine = np.polynomial.Polynomial.fit(z, np.cos(2 * np.pi * f), 7, domain=[0, 0.25]).convert()
    sine = np.polynomial.Polynomial.fit(z, np.sin(2 * np.pi * f) / f, 6, domain=[0, 0.25]).convert()
    return [float(v) for v in cosine.coef], [float(v) for v in sine.coef]


def cos_sin_turns(turns):
    cosine, sine = unit_polys()
    frac = turns - jnp.round(turns)
    z = frac * frac

    def horner(coef):
        value = jnp.full_like(z, coef[-1])
        for v in coef[-2::-1]:
            value = value * z + v
        return value

    return horner(cosine), horner(sine) * frac


def stacked(matrix):
    return np.concatenate(list(halves(matrix)), axis=-2)


def both_halves(m, value):
    count = m.shape[0] // 2
    y = dot(m, jnp.concatenate(split(value), axis=1))
    y = y[:count] + y[count:]
    return y[:, :LANES] + y[:, LANES:]


def azimuth_block(p, in_ref, par_ref, fwd_ref, inv_ref, out_ref):
    total = in_ref.shape[2]
    lead = total // LANES
    values = [
        tuple(in_ref[p, q, LANES * a : LANES * a + LANES, :].astype(f32) for q in range(2))
        for a in range(lead)
    ]
    values = fft_list(values, -1.0)
    sharp = par_ref[p, 0] * (total / 8.0)
    centre = par_ref[p, 1]
    back = []
    for c in range(lead):
        y = both_halves(fwd_ref[c], jnp.concatenate(values[c], axis=0))
        k = c + lead * lax.broadcasted_iota(jnp.int32, (LANES, 1), 0)
        u = jnp.where(k >= total // 2, k - total, k).astype(f32) * (1.0 / total)
        w = u - centre
        co, si = cos_sin_turns(sharp * w * w)
        re, im = y[:LANES], y[LANES:]
        y = both_halves(
            inv_ref[c], jnp.concatenate([re * co - im * si, re * si + im * co], axis=0)
        )
        back.append((y[:LANES], y[LANES:]))
    half = PATCH // 2
    for a, pair in enumerate(fft_list(back, 1.0)):
        for q in range(2):
            value = (pair[q] * (1.0 / total)).astype(bf16).astype(f32)
            out_ref[p, q, LANES * a + half : LANES * a + half + LANES, :] = value


LAG = 6
HEAD = 3


def focus_body(
    names, sizes, valid_hbm, root_hbm, off_hbm, echo_hbm, filt_in, slope_ref, centre_ref,
    tw_ref, ph_ref, rf_ref, ri_ref, af_hbm, ai_hbm, fr_hbm, ir_hbm, fl_hbm, il_hbm, ones_hbm,
    out_ref, valid_ref, root_ref, off_ref, echo_ref, af_ref, ai_ref, fr_ref, ir_ref, fl_ref,
    il_ref, ones_ref, filt_ref, par_ref, edge, zh, zl, comp, turned, image,
    halo_out, halo_in, crop, pass_up, pass_down, from_up, from_down, stack, power, surface, give_sem, small_sem, echo_sem, const_sem, send_sem, recv_sem, edge_send, edge_recv,
    halo_send, halo_recv, up_send, up_recv, down_send, down_recv,
):
    here = {name: lax.axis_index(name) for name in names}
    me, peers = here["lines"], sizes["lines"]
    spot, stack_size = here["acq"], sizes["acq"]
    rows, length = echo_ref.shape[1:]
    lead = length // LANES
    pairs = turned.shape[0] // 2
    total = turned.shape[2]
    row_blocks = total // LANES
    half = PATCH // 2
    block = rows // echo_sem.shape[0]
    blocks = rows // block

    small = [
        pltpu.make_async_copy(src, dst, small_sem.at[n])
        for n, (src, dst) in enumerate(
            [(valid_hbm, valid_ref), (root_hbm, root_ref), (off_hbm, off_ref)]
        )
    ]
    consts = [
        pltpu.make_async_copy(src, dst, const_sem.at[n])
        for n, (src, dst) in enumerate([
            (af_hbm, af_ref), (ai_hbm, ai_ref), (fr_hbm, fr_ref), (ir_hbm, ir_ref),
            (fl_hbm, fl_ref), (il_hbm, il_ref), (ones_hbm, ones_ref),
        ])
    ]

    def load(b):
        at = pl.ds(pl.multiple_of(b * block, block), block)
        return pltpu.make_async_copy(
            echo_hbm.at[0, :, at, :], echo_ref.at[:, at, :], echo_sem.at[b]
        )

    small[0].start()
    for b in range(blocks):
        load(b).start()
    for copy in small[1:] + consts:
        copy.start()

    def device(axis, index):
        return tuple(index if name == axis else here[name] for name in names)

    def remote(src, dst, send, recv, axis, index):
        return pltpu.make_async_remote_copy(
            src_ref=src, dst_ref=dst, send_sem=send, recv_sem=recv,
            device_id=device(axis, index), device_id_type=pl.DeviceIdType.MESH,
        )

    barrier = pltpu.get_barrier_semaphore()
    targets = [("lines", (me + d) % peers) for d in range(1, peers)]
    targets += [("acq", (spot + d) % stack_size) for d in (1, stack_size - 1)]
    for axis, index in targets:
        pl.semaphore_signal(
            barrier, inc=1, device_id=device(axis, index), device_id_type=pl.DeviceIdType.MESH
        )

    per = LANES // lead
    parts = []
    for q in range(2):
        v = jnp.concatenate(
            [filt_in[0, q : q + 1, LANES * r : LANES * r + LANES] for r in range(lead)], axis=0
        ).T
        parts.append(
            jnp.concatenate([v[lead * m : lead * m + lead] for m in range(per)], axis=1)
        )
    filt_ref[0] = parts[0] * ph_ref[0] - parts[1] * ph_ref[1]
    filt_ref[1] = parts[0] * ph_ref[1] + parts[1] * ph_ref[0]

    right, left_of = (me + 1) % peers, (me + peers - 1) % peers
    edges = [
        remote(
            ref.at[:, pl.ds(0, LANES)], edge.at[n], edge_send.at[n], edge_recv.at[n],
            "lines", left_of,
        )
        for n, ref in enumerate((slope_ref, centre_ref))
    ]

    ahead = max(0, LAG * (stack_size - 2) - row_blocks - 4)
    opening = pairs - 1
    near_last = row_blocks * (pairs - 1) >= row_blocks + 1 + ahead
    early = pairs - 1 if near_last else pairs
    head = min(early, HEAD)
    order = sorted(range(1, peers), key=lambda d: -min(d, peers - d))

    def exchange(d, wave, first, count, r0, size):
        to = (me + d) % peers
        own = pl.ds(first, count)
        return remote(
            comp.at[to, own, :, pl.ds(r0, size), :],
            turned.at[own, :, pl.ds(pl.multiple_of(me * rows + r0, size), size), :],
            send_sem.at[0], recv_sem.at[wave], "lines", to,
        )

    def send_block(r0):
        for d in order:
            exchange(d, 0, 0, head, r0, block).start()

    def part_at(t):
        late = jnp.where(jnp.logical_and(t == early + 1, early < pairs), pairs - 1, t - 1)
        return jnp.where(t < early, t, jnp.where(t == early, 2 * pairs - 1, late))

    def send_part(t):
        p = part_at(t)
        for d in order:
            exchange(d, t - head + 1, p, 1, 0, rows).start()

    small[0].wait()

    def compress(b, carry):
        r0 = pl.multiple_of(b * block, block)
        load(b).wait()
        range_block(
            r0, block, me * rows, valid_ref[0], echo_ref, filt_ref, tw_ref, rf_ref, ri_ref,
            comp, zh, zl,
        )
        turned[:, :, pl.ds(pl.multiple_of(me * rows + r0, block), block), :] = comp[
            me, :, :, pl.ds(r0, block), :
        ]

        @pl.when(b == 0)
        def _():
            pl.semaphore_wait(barrier, len(targets))

        send_block(r0)
        return carry

    lax.fori_loop(0, blocks, compress, 0)
    for copy in edges:
        copy.start()

    send_part(head)

    image[:, :, :half, :] = jnp.zeros((2 * pairs + 1, 2, half, LANES), f32)
    image[:, :, half + total :, :] = jnp.zeros((2 * pairs + 1, 2, half, LANES), f32)

    @pl.when(spot == 0)
    def _():
        from_up[...] = jnp.zeros_like(from_up)

    @pl.when(spot == stack_size - 1)
    def _():
        from_down[...] = jnp.zeros_like(from_down)

    for copy in small[1:] + consts:
        copy.wait()
    for copy in edges:
        copy.wait_recv()
    lane = lax.broadcasted_iota(jnp.int32, (1, LANES), 1)
    for n, ref in enumerate((slope_ref, centre_ref)):
        row = [
            pltpu.roll(ref[:, LANES * a : LANES * a + LANES], LANES - half, 1)
            for a in range(2 * pairs)
        ]
        row.append(pltpu.roll(edge[n], LANES - half, 1))
        row = [jnp.where(lane < LANES - half, row[a], row[a + 1]) for a in range(2 * pairs)]
        for m in range(pairs):
            even, odd = row[2 * m], row[2 * m + 1]
            par_ref[m, n] = jnp.where(lane < PATCH, even, pltpu.roll(odd, PATCH, 1))
            par_ref[pairs + m, n] = jnp.where(lane < PATCH, pltpu.roll(even, PATCH, 1), odd)

    mine = root_ref[0] == spot
    lanes = (
        (spot, from_up, pass_up, up_send, up_recv, 1),
        (stack_size - 1 - spot, from_down, pass_down, down_send, down_recv, -1),
    )

    def chain(at, src, buffer, sends, recvs, step):
        return remote(
            src.at[at], buffer.at[at], sends.at[at], recvs.at[at], "acq",
            (spot + step + stack_size) % stack_size,
        )

    def slot(s, carry):
        for depth, buffer, staged, sends, recvs, step in lanes:
            at = s - LAG * (depth - 1)

            @pl.when(jnp.logical_and(depth > 0, jnp.logical_and(at >= 0, at < pairs * row_blocks)))
            def _():
                copy = chain(at, staged, buffer, sends, recvs, step)
                copy.wait_recv()

                @pl.when(depth < stack_size - 1)
                def _():
                    staged[at] = jnp.where(mine, crop[at], buffer[at])
                    copy.start()

        return carry

    def receive(wave, count):
        got = turned.at[pl.ds(0, count), :, pl.ds(0, rows * (peers - 1)), :]
        remote(got, got, send_sem.at[0], recv_sem.at[wave], "lines", right).wait_recv()

    wide_lane = lax.broadcasted_iota(jnp.int32, (LANES, LANES), 1)
    low = wide_lane < PATCH
    halo = remote(halo_out, halo_in, halo_send.at[0], halo_recv.at[0], "lines", right)

    def near(m):
        def start(a, carry):
            at = m * row_blocks + a
            line = pl.ds(pl.multiple_of(a * LANES + PATCH, PATCH), PATCH)
            for q in range(2):
                crop[at, q] = image[m, q, line, :].astype(bf16)
            for depth, buffer, staged, sends, recvs, step in lanes:
                @pl.when(jnp.logical_and(depth == 0, stack_size > 1))
                def _():
                    chain(at, crop, buffer, sends, recvs, step).start()
            return carry

        lax.fori_loop(0, row_blocks, start, 0)

    def far():
        p = 2 * pairs - 1
        for q in range(2):
            for a in range(row_blocks // 2):
                at = slice(LANES * a, LANES * a + LANES)
                above = slice(LANES * a + half, LANES * a + half + LANES)
                below = slice(above.start + total // 2, above.stop + total // 2)
                halo_out[q, at, :] = jnp.where(
                    low, pltpu.roll(image[p, q, above, :], PATCH, 1), image[p, q, below, :]
                ).astype(bf16)
        halo.start()

        @pl.when(me == peers - 1)
        def _():
            for q in range(2):
                for a in range(row_blocks):
                    at = slice(LANES * a + half, LANES * a + half + LANES)
                    image[p, q, at, :] = jnp.where(
                        wide_lane < LANES - half, image[p, q, at, :], 0.0
                    )

    def take_halo():
        halo.wait_recv()
        outside = jnp.logical_and(wide_lane < LANES - half, me == 0)
        for q in range(2):
            for a in range(row_blocks // 2):
                value = halo_in[q, LANES * a : LANES * a + LANES, :].astype(f32)
                to = half + LANES * a
                image[2 * pairs, q, to : to + LANES, :] = jnp.where(
                    outside, 0.0, pltpu.roll(value, PATCH, 1)
                )
                to += total // 2
                image[2 * pairs, q, to : to + LANES, :] = jnp.where(outside, 0.0, value)

    patch_lane = lax.broadcasted_iota(jnp.int32, (PATCH, LANES), 1)

    def put(i, kind, pair):
        at = pl.ds(pl.multiple_of(PATCH * (kind * row_blocks + i), PATCH), PATCH)
        for q in range(2):
            stack[at, LANES * q : LANES * q + LANES] = pair[q].astype(bf16)
        re, im = pair
        power[pl.ds(kind * row_blocks + i, 1), :] = jnp.sum(re * re + im * im, axis=0, keepdims=True)

    def window(m, i):
        picked = []
        for s in range(2):
            across = off_ref[0, 1, i, 2 * m + s]
            down = pl.ds(LANES * i + PATCH + off_ref[0, 0, i, 2 * m + s], PATCH)
            back = across < 0
            turn = across + jnp.where(back, PATCH, 0)
            before = pairs + m if s else jnp.where(m == 0, 2 * pairs, pairs + m - 1)
            first = jnp.where(back, before, m)
            second = jnp.where(back, m, pairs + m)
            base = jnp.where(back, PATCH * (1 - s), PATCH * s)
            start = patch_lane - PATCH * s < PATCH - turn
            picked.append([
                jnp.where(
                    start,
                    pltpu.roll(
                        image[first, q, down, :], (2 * LANES + PATCH * s - base - turn) % LANES, 1
                    ),
                    pltpu.roll(image[second, q, down, :], (PATCH + LANES - turn) % LANES, 1),
                )
                for q in range(2)
            ])
        return [jnp.where(patch_lane < PATCH, picked[0][q], picked[1][q]) for q in range(2)]

    def left(m_ref, value):
        y = dot(m_ref[...], value.astype(bf16))
        return y[:LANES] + y[LANES:]

    def right_product(value, m_ref):
        return dot(value, m_ref[0]) + dot(value, m_ref[1])

    def give(m):
        to = pl.ds(pl.multiple_of(m * LANES, LANES), LANES)
        return pltpu.make_async_copy(
            surface.at[:, :, to], out_ref.at[0, :, :, to], give_sem.at[m]
        )

    def correlate(m):
        def one(i, carry):
            put(i, 1, window(m, i))
            at = m * row_blocks + i
            put(i, 0, [
                jnp.where(
                    mine, crop[at, q],
                    jnp.where(root_ref[0] < spot, from_up[at, q], from_down[at, q]),
                ).astype(f32)
                for q in range(2)
            ])
            return carry

        lax.fori_loop(0, row_blocks, one, 0)
        y = right_product(stack[...], fr_ref)
        z = left(fl_ref, jnp.concatenate([
            jnp.concatenate(
                [
                    y[PATCH * n : PATCH * n + PATCH, LANES * q : LANES * q + LANES]
                    for n in range(2 * row_blocks)
                ],
                axis=1,
            )
            for q in range(2)
        ], axis=0))
        z, zs = z[:, : LANES * row_blocks], z[:, LANES * row_blocks :]
        pr, pi, sr, si = z[:PATCH], z[PATCH:], zs[:PATCH], zs[PATCH:]
        x = left(il_ref, jnp.concatenate([pr * sr + pi * si, pi * sr - pr * si], axis=0))
        x = jnp.concatenate([
            jnp.concatenate(
                [
                    x[PATCH * q : PATCH * q + PATCH, LANES * n : LANES * n + LANES]
                    for n in range(row_blocks)
                ],
                axis=0,
            )
            for q in range(2)
        ], axis=1)
        y = right_product(x.astype(bf16), ir_ref)
        means = jnp.dot(
            power[...], ones_ref[...], precision=lax.Precision.HIGHEST, preferred_element_type=f32
        )
        scale = lax.rsqrt(means + eps)
        factor = scale[:row_blocks] * scale[row_blocks:] * (1.0 / PATCH**3)
        to = pl.ds(pl.multiple_of(m * LANES, LANES), LANES)
        for i in range(row_blocks):
            for q in range(2):
                surface[q, PATCH * i : PATCH * i + PATCH, to] = (
                    y[PATCH * i : PATCH * i + PATCH, LANES * q : LANES * q + LANES]
                    * factor[i : i + 1, :]
                )
        give(m).start()

    def slots(t, first, count):
        @pl.when(t >= opening)
        def _():
            at = (row_blocks + 1) * (t - opening)
            start = jnp.where(jnp.logical_and(t == opening, first <= 0), 0, at + first + ahead)
            stop = jnp.where(jnp.logical_and(t == opening, first < 0), 0, at + first + count + ahead)
            lax.fori_loop(start, stop, slot, 0)

    def step(t, carry):
        slots(t, -1, 1)

        @pl.when(t < 2 * pairs)
        def _():
            p = part_at(t)

            @pl.when(t == 0)
            def _():
                receive(0, head)

            @pl.when(t >= head)
            def _():
                receive(t - head + 1, 1)

            @pl.when(jnp.logical_and(jnp.logical_or(t == 0, t >= head), t < 2 * pairs - 2))
            def _():
                send_part(jnp.where(t == 0, head + 1, t + 2))

            azimuth_block(p, turned, par_ref, af_ref, ai_ref, image)

            @pl.when(p < pairs)
            def _():
                near(p)

            @pl.when(t == early)
            def _():
                far()

        slots(t, 0, 2)

        @pl.when(t > pairs)
        def _():
            @pl.when(t == pairs + 1)
            def _():
                take_halo()

            correlate(t - pairs - 1)

        slots(t, 2, 2)
        return carry

    lax.fori_loop(0, 2 * pairs + 1, step, 0)

    for depth, buffer, staged, sends, recvs, step_by in lanes:

        @pl.when(depth < stack_size - 1)
        def _():
            lax.fori_loop(
                0, pairs * row_blocks,
                lambda n, x: (chain(n, staged, buffer, sends, recvs, step_by).wait_send(), x)[1], 0,
            )

    halo.wait_send()
    for copy in edges:
        copy.wait_send()

    lax.fori_loop(0, pairs, lambda m, x: (give(m).wait(), x)[1], 0)
    sent = comp.at[pl.ds(0, peers - 1)]
    remote(sent, sent, send_sem.at[0], recv_sem.at[0], "lines", right).wait_send()


def focus(names, sizes, valid, root, echo, filt, slope, centre, offsets):
    rows, length = echo.shape[2:]
    lead = length // LANES
    block = min(rows, 32)
    blocks = rows // block
    total, cols = rows * sizes["lines"], slope.shape[1]
    peers = sizes["lines"]
    wide = 2 * LANES
    pairs = cols // wide
    row_blocks = total // LANES
    half = PATCH // 2
    place = np.arange(LANES)
    per = LANES // lead
    freq = per * (place % lead) + place // lead
    rf = halves(right_form(dft(LANES, -1.0)[:, freq]))
    ri = halves(right_form(dft(LANES, 1.0)[freq, :]))
    angle = 2 * np.pi * np.outer(np.arange(lead), place) / length
    tw = np.stack([np.cos(angle), -np.sin(angle)]).astype(np.float32)
    whole = np.arange(lead)[:, None] + lead * freq[None, :]
    angle = 2 * np.pi * ((half * whole) % length) / length
    ph = (np.stack([np.cos(angle), np.sin(angle)]) / length).astype(np.float32)
    fwd, inv = [], []
    for c in range(row_blocks):
        phase = np.exp(-2j * np.pi * c * place / total)
        matrix = dft(LANES, -1.0) * phase[None, :]
        fwd.append(left_form(matrix))
        inv.append(left_form(matrix.conj().T))
    fwd, inv = stacked(np.stack(fwd)), stacked(np.stack(inv))
    two = np.eye(2)
    fr = halves(right_form(np.kron(two, dft(PATCH, -1.0))))
    ir = halves(right_form(np.kron(two, dft(PATCH, 1.0))))
    fl = stacked(left_form(dft(PATCH, -1.0)))
    il = stacked(left_form(dft(PATCH, 1.0)))
    ones = np.kron(two, np.full((PATCH, PATCH), 1.0 / PATCH**2)).astype(np.float32)
    hbm, vmem = pl.BlockSpec(memory_space=pl.ANY), pl.BlockSpec(memory_space=pltpu.VMEM)
    dma = pltpu.SemaphoreType.DMA
    chunk = pltpu.VMEM((pairs * row_blocks, 2, PATCH, LANES), bf16)
    consts = (fwd, inv, fr, ir, fl, il, ones)
    return pl.pallas_call(
        functools.partial(focus_body, names, sizes),
        in_specs=[hbm] * 4 + [vmem] * 7 + [hbm] * 7,
        out_specs=hbm,
        out_shape=jax.ShapeDtypeStruct((1, 2, total // 2, cols // 2), f32),
        scratch_shapes=[
            pltpu.SMEM(valid.shape, jnp.int32),
            pltpu.SMEM(root.shape, jnp.int32),
            pltpu.SMEM(offsets.shape, jnp.int32),
            pltpu.VMEM((2, rows, length), bf16),
        ]
        + [pltpu.VMEM(c.shape, c.dtype) for c in consts]
        + [
            pltpu.VMEM((2, lead, LANES), f32),
            pltpu.VMEM((2 * pairs, 2, 1, LANES), f32),
            pltpu.VMEM((2, 1, LANES), f32),
            pltpu.VMEM((lead * block, wide), bf16),
            pltpu.VMEM((lead * block, wide), bf16),
            pltpu.VMEM((peers, 2 * pairs, 2, rows, LANES), bf16),
            pltpu.VMEM((2 * pairs, 2, total, LANES), bf16),
            pltpu.VMEM((2 * pairs + 1, 2, total + PATCH, LANES), f32),
            pltpu.VMEM((2, total // 2, LANES), bf16),
            pltpu.VMEM((2, total // 2, LANES), bf16),
        ]
        + [chunk] * 5
        + [
            pltpu.VMEM((2 * row_blocks * PATCH, wide), bf16),
            pltpu.VMEM((2 * row_blocks, LANES), f32),
            pltpu.VMEM((2, total // 2, cols // 2), f32),
            dma((pairs,)),
        ]
        + [dma((3,)), dma((blocks,)), dma((len(consts),))]
        + [dma((1,)), dma((2 * pairs,))]
        + [dma((2,))] * 2
        + [dma((1,))] * 2
        + [dma((pairs * row_blocks,))] * 4,
        compiler_params=pltpu.CompilerParams(
            collective_id=0, has_side_effects=True, vmem_limit_bytes=63 * 1024 * 1024
        ),
        name="focus",
    )(valid, root, offsets, echo, filt, slope, centre, tw, ph, rf, ri, *consts)


def on_device(names, sizes, echo, filt, slope, centre, valid, reference_index, offsets):
    return focus(names, sizes, valid, reference_index, echo, filt, slope, centre, offsets)


def solution(mesh):
    names = tuple(mesh.axis_names)
    sizes = {name: int(mesh.shape[name]) for name in names}
    return jax.shard_map(
        functools.partial(on_device, names, sizes),
        mesh=mesh,
        in_specs=(
            P(("stack", "acq"), None, "lines", None),
            P(("stack", "acq"), None, None),
            P(("stack", "acq"), "lines"),
            P(("stack", "acq"), "lines"),
            P(("stack", "acq")),
            P("stack"),
            P(("stack", "acq"), None, None, "lines"),
        ),
        out_specs=P(("stack", "acq"), None, None, "lines"),
        check_vma=False,
    )
```

```python
import functools
import math

import jax
import jax.numpy as jnp
import numpy as np
from jax import lax
from jax.experimental import pallas as pl
from jax.experimental.pallas import tpu as pltpu
from jax.sharding import PartitionSpec as P

PATCH = 64
LANES = 128
eps = 1e-06
bf16 = jnp.bfloat16
f32 = jnp.float32


def dft(size, sign):
    index = np.arange(size)
    angle = 2.0 * np.pi * (np.outer(index, index) % size) / size
    return np.cos(angle) + 1j * sign * np.sin(angle)


def right_form(matrix):
    return np.block([[matrix.real, matrix.imag], [-matrix.imag, matrix.real]])


def left_form(matrix):
    return np.block([[matrix.real, -matrix.imag], [matrix.imag, matrix.real]])


def halves(matrix):
    high = np.asarray(matrix, np.float32).astype(bf16)
    low = (np.asarray(matrix, np.float64) - high.astype(np.float64)).astype(bf16)
    return np.stack([high, low])


def split(value):
    high = value.astype(bf16)
    return high, (value - high.astype(f32)).astype(bf16)


def dot(a, b):
    return jnp.dot(a, b, preferred_element_type=f32)


def dot_nt(a, b):
    return lax.dot_general(a, b, (((1,), (1,)), ((), ())), preferred_element_type=f32)


def dot_tn(a, b):
    return lax.dot_general(a, b, (((0,), (0,)), ((), ())), preferred_element_type=f32)


def fft_list(values, sign):
    count = len(values)
    if count == 1:
        return values
    even = fft_list(values[0::2], sign)
    odd = fft_list(values[1::2], sign)
    out = [None] * count
    for k in range(count // 2):
        re, im = odd[k]
        if k == 0:
            pass
        elif 4 * k == count:
            re, im = (-im, re) if sign > 0 else (im, -re)
        elif 8 * k == count:
            r = math.sqrt(0.5)
            re, im = ((re - im) * r, (re + im) * r) if sign > 0 else ((re + im) * r, (im - re) * r)
        elif 8 * k == 3 * count:
            r = math.sqrt(0.5)
            re, im = ((re + im) * -r, (re - im) * r) if sign > 0 else ((im - re) * r, (re + im) * -r)
        else:
            c = math.cos(2 * math.pi * k / count)
            s = sign * math.sin(2 * math.pi * k / count)
            re, im = re * c - im * s, re * s + im * c
        out[k] = (even[k][0] + re, even[k][1] + im)
        out[k + count // 2] = (even[k][0] - re, even[k][1] - im)
    return out


def range_block(r0, block, first, valid, echo_ref, filt_ref, tw_ref, fwd_ref, inv_ref, out_ref, zh, zl):
    lead = echo_ref.shape[2] // LANES
    peers, pairs = out_ref.shape[0], out_ref.shape[1] // 2
    group = 16
    low = lax.broadcasted_iota(jnp.int32, (group, LANES), 1) < PATCH

    def put(row, count, re, im):
        zh[row : row + count, :LANES], zl[row : row + count, :LANES] = split(re)
        zh[row : row + count, LANES:], zl[row : row + count, LANES:] = split(im)

    def product(m_ref):
        h = zh[...]
        return dot(h, m_ref[0]) + dot(zl[...], m_ref[0]) + dot(h, m_ref[1])

    for g in range(block // group):
        at = pl.multiple_of(r0 + g * group, group)
        line = first + at + lax.broadcasted_iota(jnp.int32, (group, 1), 0)
        keep = (line < valid).astype(f32)
        values = [
            tuple(
                echo_ref[q, pl.ds(at, group), LANES * a : LANES * a + LANES].astype(f32) * keep
                for q in range(2)
            )
            for a in range(lead)
        ]
        for c, (re, im) in enumerate(fft_list(values, -1.0)):
            tr, ti = tw_ref[0, c : c + 1, :], tw_ref[1, c : c + 1, :]
            put(c * block + g * group, group, re * tr - im * ti, re * ti + im * tr)
    y = product(fwd_ref)
    for c in range(lead):
        part = y[c * block : c * block + block]
        re, im = part[:, :LANES], part[:, LANES:]
        hr, hi = filt_ref[0, c : c + 1, :], filt_ref[1, c : c + 1, :]
        put(c * block, block, re * hr - im * hi, re * hi + im * hr)
    y = product(inv_ref)
    for g in range(block // group):
        at = pl.multiple_of(r0 + g * group, group)
        values = []
        for c in range(lead):
            part = y[c * block + g * group : c * block + g * group + group]
            re, im = part[:, :LANES], part[:, LANES:]
            tr, ti = tw_ref[0, c : c + 1, :], tw_ref[1, c : c + 1, :]
            values.append((re * tr + im * ti, im * tr - re * ti))
        values = fft_list(values, 1.0)
        for t in range(lead // 2):
            for q in range(2):
                even, odd = values[2 * t][q], values[2 * t + 1][q]
                near = jnp.where(low, even, pltpu.roll(odd, PATCH, 1))
                far = jnp.where(low, pltpu.roll(even, PATCH, 1), odd)
                to, m = divmod(t, pairs)
                out_ref[to, m, q, pl.ds(at, group), :] = near.astype(bf16)
                out_ref[to, pairs + m, q, pl.ds(at, group), :] = far.astype(bf16)


def unit_polys():
    z = 0.125 - 0.125 * np.cos(np.pi * (np.arange(400) + 0.5) / 400)
    f = np.sqrt(z)
    cosine = np.polynomial.Polynomial.fit(z, np.cos(2 * np.pi * f), 7, domain=[0, 0.25]).convert()
    sine = np.polynomial.Polynomial.fit(z, np.sin(2 * np.pi * f) / f, 6, domain=[0, 0.25]).convert()
    return [float(v) for v in cosine.coef], [float(v) for v in sine.coef]


def cos_sin_turns(turns):
    cosine, sine = unit_polys()
    frac = turns - jnp.round(turns)
    z = frac * frac

    def horner(coef):
        value = jnp.full_like(z, coef[-1])
        for v in coef[-2::-1]:
            value = value * z + v
        return value

    return horner(cosine), horner(sine) * frac


def stacked(matrix):
    return np.concatenate(list(halves(matrix)), axis=-2)


def both_halves(m, value):
    count = m.shape[0] // 2
    y = dot(m, jnp.concatenate(split(value), axis=1))
    y = y[:count] + y[count:]
    return y[:, :LANES] + y[:, LANES:]


def azimuth_block(p, in_ref, par_ref, fwd_ref, inv_ref, out_ref):
    total = in_ref.shape[2]
    lead = total // LANES
    values = [
        tuple(in_ref[p, q, LANES * a : LANES * a + LANES, :].astype(f32) for q in range(2))
        for a in range(lead)
    ]
    values = fft_list(values, -1.0)
    sharp = par_ref[p, 0] * (total / 8.0)
    centre = par_ref[p, 1]
    back = []
    for c in range(lead):
        y = both_halves(fwd_ref[c], jnp.concatenate(values[c], axis=0))
        k = c + lead * lax.broadcasted_iota(jnp.int32, (LANES, 1), 0)
        u = jnp.where(k >= total // 2, k - total, k).astype(f32) * (1.0 / total)
        w = u - centre
        co, si = cos_sin_turns(sharp * w * w)
        re, im = y[:LANES], y[LANES:]
        y = both_halves(
            inv_ref[c], jnp.concatenate([re * co - im * si, re * si + im * co], axis=0)
        )
        back.append((y[:LANES], y[LANES:]))
    half = PATCH // 2
    for a, pair in enumerate(fft_list(back, 1.0)):
        for q in range(2):
            value = (pair[q] * (1.0 / total)).astype(bf16).astype(f32)
            out_ref[p, q, LANES * a + half : LANES * a + half + LANES, :] = value


LAG = 5
HEAD = 3


def focus_body(
    names, sizes, valid_hbm, root_hbm, off_hbm, echo_hbm, filt_in, slope_ref, centre_ref,
    tw_ref, ph_ref, rf_ref, ri_ref, af_hbm, ai_hbm, fr_hbm, ir_hbm, fl_hbm, il_hbm, ones_hbm,
    out_ref, valid_ref, root_ref, off_ref, echo_ref, af_ref, ai_ref, fr_ref, ir_ref, fl_ref,
    il_ref, ones_ref, filt_ref, par_ref, edge, zh, zl, comp, turned, image,
    halo_out, halo_in, crop, pass_up, pass_down, from_up, from_down, stack, power, surface, give_sem, small_sem, echo_sem, const_sem, send_sem, recv_sem, edge_send, edge_recv,
    halo_send, halo_recv, up_send, up_recv, down_send, down_recv,
):
    here = {name: lax.axis_index(name) for name in names}
    me, peers = here["lines"], sizes["lines"]
    spot, stack_size = here["acq"], sizes["acq"]
    rows, length = echo_ref.shape[1:]
    lead = length // LANES
    pairs = turned.shape[0] // 2
    total = turned.shape[2]
    row_blocks = total // LANES
    half = PATCH // 2
    block = rows // echo_sem.shape[0]
    blocks = rows // block

    small = [
        pltpu.make_async_copy(src, dst, small_sem.at[n])
        for n, (src, dst) in enumerate(
            [(valid_hbm, valid_ref), (root_hbm, root_ref), (off_hbm, off_ref)]
        )
    ]
    consts = [
        pltpu.make_async_copy(src, dst, const_sem.at[n])
        for n, (src, dst) in enumerate([
            (af_hbm, af_ref), (ai_hbm, ai_ref), (fr_hbm, fr_ref), (ir_hbm, ir_ref),
            (fl_hbm, fl_ref), (il_hbm, il_ref), (ones_hbm, ones_ref),
        ])
    ]

    def load(b):
        at = pl.ds(pl.multiple_of(b * block, block), block)
        return pltpu.make_async_copy(
            echo_hbm.at[0, :, at, :], echo_ref.at[:, at, :], echo_sem.at[b]
        )

    small[0].start()
    for b in range(blocks):
        load(b).start()
    for copy in small[1:] + consts:
        copy.start()

    def device(axis, index):
        return tuple(index if name == axis else here[name] for name in names)

    def remote(src, dst, send, recv, axis, index):
        return pltpu.make_async_remote_copy(
            src_ref=src, dst_ref=dst, send_sem=send, recv_sem=recv,
            device_id=device(axis, index), device_id_type=pl.DeviceIdType.MESH,
        )

    barrier = pltpu.get_barrier_semaphore()
    targets = [("lines", (me + d) % peers) for d in range(1, peers)]
    targets += [("acq", (spot + d) % stack_size) for d in (1, stack_size - 1)]
    for axis, index in targets:
        pl.semaphore_signal(
            barrier, inc=1, device_id=device(axis, index), device_id_type=pl.DeviceIdType.MESH
        )

    per = LANES // lead
    parts = []
    for q in range(2):
        v = jnp.concatenate(
            [filt_in[0, q : q + 1, LANES * r : LANES * r + LANES] for r in range(lead)], axis=0
        ).T
        parts.append(
            jnp.concatenate([v[lead * m : lead * m + lead] for m in range(per)], axis=1)
        )
    filt_ref[0] = parts[0] * ph_ref[0] - parts[1] * ph_ref[1]
    filt_ref[1] = parts[0] * ph_ref[1] + parts[1] * ph_ref[0]

    right, left_of = (me + 1) % peers, (me + peers - 1) % peers
    edges = [
        remote(
            ref.at[:, pl.ds(0, LANES)], edge.at[n], edge_send.at[n], edge_recv.at[n],
            "lines", left_of,
        )
        for n, ref in enumerate((slope_ref, centre_ref))
    ]

    ahead = max(0, LAG * (stack_size - 2) - row_blocks - 4)
    opening = pairs - 1
    near_last = row_blocks * (pairs - 1) >= row_blocks + 1 + ahead
    early = pairs - 1 if near_last else pairs
    head = min(early, HEAD)
    order = sorted(range(1, peers), key=lambda d: -min(d, peers - d))

    def exchange(d, wave, first, count, r0, size):
        to = (me + d) % peers
        own = pl.ds(first, count)
        return remote(
            comp.at[to, own, :, pl.ds(r0, size), :],
            turned.at[own, :, pl.ds(pl.multiple_of(me * rows + r0, size), size), :],
            send_sem.at[0], recv_sem.at[wave], "lines", to,
        )

    def send_block(r0):
        for d in order:
            exchange(d, 0, 0, head, r0, block).start()

    def part_at(t):
        late = jnp.where(jnp.logical_and(t == early + 1, early < pairs), pairs - 1, t - 1)
        return jnp.where(t < early, t, jnp.where(t == early, 2 * pairs - 1, late))

    def send_part(t):
        p = part_at(t)
        for d in order:
            exchange(d, t - head + 1, p, 1, 0, rows).start()

    small[0].wait()

    def compress(b, carry):
        r0 = pl.multiple_of(b * block, block)
        load(b).wait()
        range_block(
            r0, block, me * rows, valid_ref[0], echo_ref, filt_ref, tw_ref, rf_ref, ri_ref,
            comp, zh, zl,
        )
        turned[:, :, pl.ds(pl.multiple_of(me * rows + r0, block), block), :] = comp[
            me, :, :, pl.ds(r0, block), :
        ]

        @pl.when(b == 0)
        def _():
            pl.semaphore_wait(barrier, len(targets))

        send_block(r0)
        return carry

    lax.fori_loop(0, blocks, compress, 0)
    for copy in edges:
        copy.start()

    send_part(head)

    image[:, :, :half, :] = jnp.zeros((2 * pairs + 1, 2, half, LANES), f32)
    image[:, :, half + total :, :] = jnp.zeros((2 * pairs + 1, 2, half, LANES), f32)

    @pl.when(spot == 0)
    def _():
        from_up[...] = jnp.zeros_like(from_up)

    @pl.when(spot == stack_size - 1)
    def _():
        from_down[...] = jnp.zeros_like(from_down)

    for copy in small[1:] + consts:
        copy.wait()
    for copy in edges:
        copy.wait_recv()
    lane = lax.broadcasted_iota(jnp.int32, (1, LANES), 1)
    for n, ref in enumerate((slope_ref, centre_ref)):
        row = [
            pltpu.roll(ref[:, LANES * a : LANES * a + LANES], LANES - half, 1)
            for a in range(2 * pairs)
        ]
        row.append(pltpu.roll(edge[n], LANES - half, 1))
        row = [jnp.where(lane < LANES - half, row[a], row[a + 1]) for a in range(2 * pairs)]
        for m in range(pairs):
            even, odd = row[2 * m], row[2 * m + 1]
            par_ref[m, n] = jnp.where(lane < PATCH, even, pltpu.roll(odd, PATCH, 1))
            par_ref[pairs + m, n] = jnp.where(lane < PATCH, pltpu.roll(even, PATCH, 1), odd)

    mine = root_ref[0] == spot
    lanes = (
        (spot, from_up, pass_up, up_send, up_recv, 1),
        (stack_size - 1 - spot, from_down, pass_down, down_send, down_recv, -1),
    )

    def chain(at, src, buffer, sends, recvs, step):
        return remote(
            src.at[at], buffer.at[at], sends.at[at], recvs.at[at], "acq",
            (spot + step + stack_size) % stack_size,
        )

    def slot(s, carry):
        for depth, buffer, staged, sends, recvs, step in lanes:
            at = s - LAG * (depth - 1)

            @pl.when(jnp.logical_and(depth > 0, jnp.logical_and(at >= 0, at < pairs * row_blocks)))
            def _():
                copy = chain(at, staged, buffer, sends, recvs, step)
                copy.wait_recv()

                @pl.when(depth < stack_size - 1)
                def _():
                    staged[at] = jnp.where(mine, crop[at], buffer[at])
                    copy.start()

        return carry

    def receive(wave, count):
        got = turned.at[pl.ds(0, count), :, pl.ds(0, rows * (peers - 1)), :]
        remote(got, got, send_sem.at[0], recv_sem.at[wave], "lines", right).wait_recv()

    wide_lane = lax.broadcasted_iota(jnp.int32, (LANES, LANES), 1)
    low = wide_lane < PATCH
    halo = remote(halo_out, halo_in, halo_send.at[0], halo_recv.at[0], "lines", right)

    def near(m):
        def start(a, carry):
            at = m * row_blocks + a
            line = pl.ds(pl.multiple_of(a * LANES + PATCH, PATCH), PATCH)
            for q in range(2):
                crop[at, q] = image[m, q, line, :].astype(bf16)
            for depth, buffer, staged, sends, recvs, step in lanes:
                @pl.when(jnp.logical_and(depth == 0, stack_size > 1))
                def _():
                    chain(at, crop, buffer, sends, recvs, step).start()
            return carry

        lax.fori_loop(0, row_blocks, start, 0)

    def far():
        p = 2 * pairs - 1
        for q in range(2):
            for a in range(row_blocks // 2):
                at = slice(LANES * a, LANES * a + LANES)
                above = slice(LANES * a + half, LANES * a + half + LANES)
                below = slice(above.start + total // 2, above.stop + total // 2)
                halo_out[q, at, :] = jnp.where(
                    low, pltpu.roll(image[p, q, above, :], PATCH, 1), image[p, q, below, :]
                ).astype(bf16)
        halo.start()

        @pl.when(me == peers - 1)
        def _():
            for q in range(2):
                for a in range(row_blocks):
                    at = slice(LANES * a + half, LANES * a + half + LANES)
                    image[p, q, at, :] = jnp.where(
                        wide_lane < LANES - half, image[p, q, at, :], 0.0
                    )

    def take_halo():
        halo.wait_recv()
        outside = jnp.logical_and(wide_lane < LANES - half, me == 0)
        for q in range(2):
            for a in range(row_blocks // 2):
                value = halo_in[q, LANES * a : LANES * a + LANES, :].astype(f32)
                to = half + LANES * a
                image[2 * pairs, q, to : to + LANES, :] = jnp.where(
                    outside, 0.0, pltpu.roll(value, PATCH, 1)
                )
                to += total // 2
                image[2 * pairs, q, to : to + LANES, :] = jnp.where(outside, 0.0, value)

    patch_lane = lax.broadcasted_iota(jnp.int32, (PATCH, LANES), 1)

    def put(i, kind, pair):
        at = pl.ds(pl.multiple_of(PATCH * (kind * row_blocks + i), PATCH), PATCH)
        for q in range(2):
            stack[at, LANES * q : LANES * q + LANES] = pair[q].astype(bf16)
        re, im = pair
        power[pl.ds(kind * row_blocks + i, 1), :] = jnp.sum(re * re + im * im, axis=0, keepdims=True)

    def window(m, i):
        picked = []
        for s in range(2):
            across = off_ref[0, 1, i, 2 * m + s]
            down = pl.ds(LANES * i + PATCH + off_ref[0, 0, i, 2 * m + s], PATCH)
            back = across < 0
            turn = across + jnp.where(back, PATCH, 0)
            before = pairs + m if s else jnp.where(m == 0, 2 * pairs, pairs + m - 1)
            first = jnp.where(back, before, m)
            second = jnp.where(back, m, pairs + m)
            base = jnp.where(back, PATCH * (1 - s), PATCH * s)
            start = patch_lane - PATCH * s < PATCH - turn
            picked.append([
                jnp.where(
                    start,
                    pltpu.roll(
                        image[first, q, down, :], (2 * LANES + PATCH * s - base - turn) % LANES, 1
                    ),
                    pltpu.roll(image[second, q, down, :], (PATCH + LANES - turn) % LANES, 1),
                )
                for q in range(2)
            ])
        return [jnp.where(patch_lane < PATCH, picked[0][q], picked[1][q]) for q in range(2)]

    def left(m_ref, value):
        y = dot(m_ref[...], value.astype(bf16))
        return y[:LANES] + y[LANES:]

    def right_product(value, m_ref):
        return dot(value, m_ref[0]) + dot(value, m_ref[1])

    def give(m):
        to = pl.ds(pl.multiple_of(m * LANES, LANES), LANES)
        return pltpu.make_async_copy(
            surface.at[:, :, to], out_ref.at[0, :, :, to], give_sem.at[m]
        )

    def correlate(m):
        def one(i, carry):
            put(i, 1, window(m, i))
            at = m * row_blocks + i
            put(i, 0, [
                jnp.where(
                    mine, crop[at, q],
                    jnp.where(root_ref[0] < spot, from_up[at, q], from_down[at, q]),
                ).astype(f32)
                for q in range(2)
            ])
            return carry

        lax.fori_loop(0, row_blocks, one, 0)
        y = right_product(stack[...], fr_ref)
        z = left(fl_ref, jnp.concatenate([
            jnp.concatenate(
                [
                    y[PATCH * n : PATCH * n + PATCH, LANES * q : LANES * q + LANES]
                    for n in range(2 * row_blocks)
                ],
                axis=1,
            )
            for q in range(2)
        ], axis=0))
        z, zs = z[:, : LANES * row_blocks], z[:, LANES * row_blocks :]
        pr, pi, sr, si = z[:PATCH], z[PATCH:], zs[:PATCH], zs[PATCH:]
        x = left(il_ref, jnp.concatenate([pr * sr + pi * si, pi * sr - pr * si], axis=0))
        x = jnp.concatenate([
            jnp.concatenate(
                [
                    x[PATCH * q : PATCH * q + PATCH, LANES * n : LANES * n + LANES]
                    for n in range(row_blocks)
                ],
                axis=0,
            )
            for q in range(2)
        ], axis=1)
        y = right_product(x.astype(bf16), ir_ref)
        means = jnp.dot(
            power[...], ones_ref[...], precision=lax.Precision.HIGHEST, preferred_element_type=f32
        )
        scale = lax.rsqrt(means + eps)
        factor = scale[:row_blocks] * scale[row_blocks:] * (1.0 / PATCH**3)
        to = pl.ds(pl.multiple_of(m * LANES, LANES), LANES)
        for i in range(row_blocks):
            for q in range(2):
                surface[q, PATCH * i : PATCH * i + PATCH, to] = (
                    y[PATCH * i : PATCH * i + PATCH, LANES * q : LANES * q + LANES]
                    * factor[i : i + 1, :]
                )
        give(m).start()

    def slots(t, first, count):
        @pl.when(t >= opening)
        def _():
            at = (row_blocks + 1) * (t - opening)
            start = jnp.where(jnp.logical_and(t == opening, first <= 0), 0, at + first + ahead)
            stop = jnp.where(jnp.logical_and(t == opening, first < 0), 0, at + first + count + ahead)
            lax.fori_loop(start, stop, slot, 0)

    def step(t, carry):
        slots(t, -1, 1)

        @pl.when(t < 2 * pairs)
        def _():
            p = part_at(t)

            @pl.when(t == 0)
            def _():
                receive(0, head)

            @pl.when(t >= head)
            def _():
                receive(t - head + 1, 1)

            @pl.when(jnp.logical_and(jnp.logical_or(t == 0, t >= head), t < 2 * pairs - 2))
            def _():
                send_part(jnp.where(t == 0, head + 1, t + 2))

            azimuth_block(p, turned, par_ref, af_ref, ai_ref, image)

            @pl.when(p < pairs)
            def _():
                near(p)

            @pl.when(t == early)
            def _():
                far()

        slots(t, 0, 2)

        @pl.when(t > pairs)
        def _():
            @pl.when(t == pairs + 1)
            def _():
                take_halo()

            correlate(t - pairs - 1)

        slots(t, 2, 2)
        return carry

    lax.fori_loop(0, 2 * pairs + 1, step, 0)

    for depth, buffer, staged, sends, recvs, step_by in lanes:

        @pl.when(depth < stack_size - 1)
        def _():
            lax.fori_loop(
                0, pairs * row_blocks,
                lambda n, x: (chain(n, staged, buffer, sends, recvs, step_by).wait_send(), x)[1], 0,
            )

    halo.wait_send()
    for copy in edges:
        copy.wait_send()

    lax.fori_loop(0, pairs, lambda m, x: (give(m).wait(), x)[1], 0)
    sent = comp.at[pl.ds(0, peers - 1)]
    remote(sent, sent, send_sem.at[0], recv_sem.at[0], "lines", right).wait_send()


def focus(names, sizes, valid, root, echo, filt, slope, centre, offsets):
    rows, length = echo.shape[2:]
    lead = length // LANES
    block = min(rows, 32)
    blocks = rows // block
    total, cols = rows * sizes["lines"], slope.shape[1]
    peers = sizes["lines"]
    wide = 2 * LANES
    pairs = cols // wide
    row_blocks = total // LANES
    half = PATCH // 2
    place = np.arange(LANES)
    per = LANES // lead
    freq = per * (place % lead) + place // lead
    rf = halves(right_form(dft(LANES, -1.0)[:, freq]))
    ri = halves(right_form(dft(LANES, 1.0)[freq, :]))
    angle = 2 * np.pi * np.outer(np.arange(lead), place) / length
    tw = np.stack([np.cos(angle), -np.sin(angle)]).astype(np.float32)
    whole = np.arange(lead)[:, None] + lead * freq[None, :]
    angle = 2 * np.pi * ((half * whole) % length) / length
    ph = (np.stack([np.cos(angle), np.sin(angle)]) / length).astype(np.float32)
    fwd, inv = [], []
    for c in range(row_blocks):
        phase = np.exp(-2j * np.pi * c * place / total)
        matrix = dft(LANES, -1.0) * phase[None, :]
        fwd.append(left_form(matrix))
        inv.append(left_form(matrix.conj().T))
    fwd, inv = stacked(np.stack(fwd)), stacked(np.stack(inv))
    two = np.eye(2)
    fr = halves(right_form(np.kron(two, dft(PATCH, -1.0))))
    ir = halves(right_form(np.kron(two, dft(PATCH, 1.0))))
    fl = stacked(left_form(dft(PATCH, -1.0)))
    il = stacked(left_form(dft(PATCH, 1.0)))
    ones = np.kron(two, np.full((PATCH, PATCH), 1.0 / PATCH**2)).astype(np.float32)
    hbm, vmem = pl.BlockSpec(memory_space=pl.ANY), pl.BlockSpec(memory_space=pltpu.VMEM)
    dma = pltpu.SemaphoreType.DMA
    chunk = pltpu.VMEM((pairs * row_blocks, 2, PATCH, LANES), bf16)
    consts = (fwd, inv, fr, ir, fl, il, ones)
    return pl.pallas_call(
        functools.partial(focus_body, names, sizes),
        in_specs=[hbm] * 4 + [vmem] * 7 + [hbm] * 7,
        out_specs=hbm,
        out_shape=jax.ShapeDtypeStruct((1, 2, total // 2, cols // 2), f32),
        scratch_shapes=[
            pltpu.SMEM(valid.shape, jnp.int32),
            pltpu.SMEM(root.shape, jnp.int32),
            pltpu.SMEM(offsets.shape, jnp.int32),
            pltpu.VMEM((2, rows, length), bf16),
        ]
        + [pltpu.VMEM(c.shape, c.dtype) for c in consts]
        + [
            pltpu.VMEM((2, lead, LANES), f32),
            pltpu.VMEM((2 * pairs, 2, 1, LANES), f32),
            pltpu.VMEM((2, 1, LANES), f32),
            pltpu.VMEM((lead * block, wide), bf16),
            pltpu.VMEM((lead * block, wide), bf16),
            pltpu.VMEM((peers, 2 * pairs, 2, rows, LANES), bf16),
            pltpu.VMEM((2 * pairs, 2, total, LANES), bf16),
            pltpu.VMEM((2 * pairs + 1, 2, total + PATCH, LANES), f32),
            pltpu.VMEM((2, total // 2, LANES), bf16),
            pltpu.VMEM((2, total // 2, LANES), bf16),
        ]
        + [chunk] * 5
        + [
            pltpu.VMEM((2 * row_blocks * PATCH, wide), bf16),
            pltpu.VMEM((2 * row_blocks, LANES), f32),
            pltpu.VMEM((2, total // 2, cols // 2), f32),
            dma((pairs,)),
        ]
        + [dma((3,)), dma((blocks,)), dma((len(consts),))]
        + [dma((1,)), dma((2 * pairs,))]
        + [dma((2,))] * 2
        + [dma((1,))] * 2
        + [dma((pairs * row_blocks,))] * 4,
        compiler_params=pltpu.CompilerParams(
            collective_id=0, has_side_effects=True, vmem_limit_bytes=63 * 1024 * 1024
        ),
        name="focus",
    )(valid, root, offsets, echo, filt, slope, centre, tw, ph, rf, ri, *consts)


def on_device(names, sizes, echo, filt, slope, centre, valid, reference_index, offsets):
    return focus(names, sizes, valid, reference_index, echo, filt, slope, centre, offsets)


def solution(mesh):
    names = tuple(mesh.axis_names)
    sizes = {name: int(mesh.shape[name]) for name in names}
    return jax.shard_map(
        functools.partial(on_device, names, sizes),
        mesh=mesh,
        in_specs=(
            P(("stack", "acq"), None, "lines", None),
            P(("stack", "acq"), None, None),
            P(("stack", "acq"), "lines"),
            P(("stack", "acq"), "lines"),
            P(("stack", "acq")),
            P("stack"),
            P(("stack", "acq"), None, None, "lines"),
        ),
        out_specs=P(("stack", "acq"), None, None, "lines"),
        check_vma=False,
    )
```

```python
import functools
import math

import jax
import jax.numpy as jnp
import numpy as np
from jax import lax
from jax.experimental import pallas as pl
from jax.experimental.pallas import tpu as pltpu
from jax.sharding import PartitionSpec as P

PATCH = 64
LANES = 128
eps = 1e-06
bf16 = jnp.bfloat16
f32 = jnp.float32


def dft(size, sign):
    index = np.arange(size)
    angle = 2.0 * np.pi * (np.outer(index, index) % size) / size
    return np.cos(angle) + 1j * sign * np.sin(angle)


def right_form(matrix):
    return np.block([[matrix.real, matrix.imag], [-matrix.imag, matrix.real]])


def left_form(matrix):
    return np.block([[matrix.real, -matrix.imag], [matrix.imag, matrix.real]])


def halves(matrix):
    high = np.asarray(matrix, np.float32).astype(bf16)
    low = (np.asarray(matrix, np.float64) - high.astype(np.float64)).astype(bf16)
    return np.stack([high, low])


def split(value):
    high = value.astype(bf16)
    return high, (value - high.astype(f32)).astype(bf16)


def dot(a, b):
    return jnp.dot(a, b, preferred_element_type=f32)


def dot_nt(a, b):
    return lax.dot_general(a, b, (((1,), (1,)), ((), ())), preferred_element_type=f32)


def dot_tn(a, b):
    return lax.dot_general(a, b, (((0,), (0,)), ((), ())), preferred_element_type=f32)


def fft_list(values, sign):
    count = len(values)
    if count == 1:
        return values
    even = fft_list(values[0::2], sign)
    odd = fft_list(values[1::2], sign)
    out = [None] * count
    for k in range(count // 2):
        re, im = odd[k]
        if k == 0:
            pass
        elif 4 * k == count:
            re, im = (-im, re) if sign > 0 else (im, -re)
        elif 8 * k == count:
            r = math.sqrt(0.5)
            re, im = ((re - im) * r, (re + im) * r) if sign > 0 else ((re + im) * r, (im - re) * r)
        elif 8 * k == 3 * count:
            r = math.sqrt(0.5)
            re, im = ((re + im) * -r, (re - im) * r) if sign > 0 else ((im - re) * r, (re + im) * -r)
        else:
            c = math.cos(2 * math.pi * k / count)
            s = sign * math.sin(2 * math.pi * k / count)
            re, im = re * c - im * s, re * s + im * c
        out[k] = (even[k][0] + re, even[k][1] + im)
        out[k + count // 2] = (even[k][0] - re, even[k][1] - im)
    return out


def range_block(r0, block, first, valid, echo_ref, filt_ref, tw_ref, fwd_ref, inv_ref, out_ref, zh, zl):
    lead = echo_ref.shape[2] // LANES
    peers, pairs = out_ref.shape[0], out_ref.shape[1] // 2
    group = 16
    low = lax.broadcasted_iota(jnp.int32, (group, LANES), 1) < PATCH

    def put(row, count, re, im):
        zh[row : row + count, :LANES], zl[row : row + count, :LANES] = split(re)
        zh[row : row + count, LANES:], zl[row : row + count, LANES:] = split(im)

    def product(m_ref):
        h = zh[...]
        return dot(h, m_ref[0]) + dot(zl[...], m_ref[0]) + dot(h, m_ref[1])

    for g in range(block // group):
        at = pl.multiple_of(r0 + g * group, group)
        line = first + at + lax.broadcasted_iota(jnp.int32, (group, 1), 0)
        keep = (line < valid).astype(f32)
        values = [
            tuple(
                echo_ref[q, pl.ds(at, group), LANES * a : LANES * a + LANES].astype(f32) * keep
                for q in range(2)
            )
            for a in range(lead)
        ]
        for c, (re, im) in enumerate(fft_list(values, -1.0)):
            tr, ti = tw_ref[0, c : c + 1, :], tw_ref[1, c : c + 1, :]
            put(c * block + g * group, group, re * tr - im * ti, re * ti + im * tr)
    y = product(fwd_ref)
    for c in range(lead):
        part = y[c * block : c * block + block]
        re, im = part[:, :LANES], part[:, LANES:]
        hr, hi = filt_ref[0, c : c + 1, :], filt_ref[1, c : c + 1, :]
        put(c * block, block, re * hr - im * hi, re * hi + im * hr)
    y = product(inv_ref)
    for g in range(block // group):
        at = pl.multiple_of(r0 + g * group, group)
        values = []
        for c in range(lead):
            part = y[c * block + g * group : c * block + g * group + group]
            re, im = part[:, :LANES], part[:, LANES:]
            tr, ti = tw_ref[0, c : c + 1, :], tw_ref[1, c : c + 1, :]
            values.append((re * tr + im * ti, im * tr - re * ti))
        values = fft_list(values, 1.0)
        for t in range(lead // 2):
            for q in range(2):
                even, odd = values[2 * t][q], values[2 * t + 1][q]
                near = jnp.where(low, even, pltpu.roll(odd, PATCH, 1))
                far = jnp.where(low, pltpu.roll(even, PATCH, 1), odd)
                to, m = divmod(t, pairs)
                out_ref[to, m, q, pl.ds(at, group), :] = near.astype(bf16)
                out_ref[to, pairs + m, q, pl.ds(at, group), :] = far.astype(bf16)


def unit_polys():
    z = 0.125 - 0.125 * np.cos(np.pi * (np.arange(400) + 0.5) / 400)
    f = np.sqrt(z)
    cosine = np.polynomial.Polynomial.fit(z, np.cos(2 * np.pi * f), 7, domain=[0, 0.25]).convert()
    sine = np.polynomial.Polynomial.fit(z, np.sin(2 * np.pi * f) / f, 6, domain=[0, 0.25]).convert()
    return [float(v) for v in cosine.coef], [float(v) for v in sine.coef]


def cos_sin_turns(turns):
    cosine, sine = unit_polys()
    frac = turns - jnp.round(turns)
    z = frac * frac

    def horner(coef):
        value = jnp.full_like(z, coef[-1])
        for v in coef[-2::-1]:
            value = value * z + v
        return value

    return horner(cosine), horner(sine) * frac


def stacked(matrix):
    return np.concatenate(list(halves(matrix)), axis=-2)


def both_halves(m, value):
    count = m.shape[0] // 2
    y = dot(m, jnp.concatenate(split(value), axis=1))
    y = y[:count] + y[count:]
    return y[:, :LANES] + y[:, LANES:]


def azimuth_block(p, in_ref, par_ref, fwd_ref, inv_ref, out_ref):
    total = in_ref.shape[2]
    lead = total // LANES
    values = [
        tuple(in_ref[p, q, LANES * a : LANES * a + LANES, :].astype(f32) for q in range(2))
        for a in range(lead)
    ]
    values = fft_list(values, -1.0)
    sharp = par_ref[p, 0] * (total / 8.0)
    centre = par_ref[p, 1]
    back = []
    for c in range(lead):
        y = both_halves(fwd_ref[c], jnp.concatenate(values[c], axis=0))
        k = c + lead * lax.broadcasted_iota(jnp.int32, (LANES, 1), 0)
        u = jnp.where(k >= total // 2, k - total, k).astype(f32) * (1.0 / total)
        w = u - centre
        co, si = cos_sin_turns(sharp * w * w)
        re, im = y[:LANES], y[LANES:]
        y = both_halves(
            inv_ref[c], jnp.concatenate([re * co - im * si, re * si + im * co], axis=0)
        )
        back.append((y[:LANES], y[LANES:]))
    half = PATCH // 2
    for a, pair in enumerate(fft_list(back, 1.0)):
        for q in range(2):
            value = (pair[q] * (1.0 / total)).astype(bf16).astype(f32)
            out_ref[p, q, LANES * a + half : LANES * a + half + LANES, :] = value


LAG = 5
HEAD = 3


def focus_body(
    names, sizes, valid_hbm, root_hbm, off_hbm, echo_hbm, filt_in, slope_ref, centre_ref,
    tw_ref, ph_ref, rf_ref, ri_ref, af_hbm, ai_hbm, fr_hbm, ir_hbm, fl_hbm, il_hbm,
    out_ref, valid_ref, root_ref, off_ref, echo_ref, af_ref, ai_ref, fr_ref, ir_ref, fl_ref,
    il_ref, filt_ref, par_ref, edge, zh, zl, comp, turned, image,
    halo_out, halo_in, crop, pass_up, pass_down, from_up, from_down, stack, power, surface, give_sem, small_sem, echo_sem, const_sem, send_sem, recv_sem, edge_send, edge_recv,
    halo_send, halo_recv, up_send, up_recv, down_send, down_recv,
):
    here = {name: lax.axis_index(name) for name in names}
    me, peers = here["lines"], sizes["lines"]
    spot, stack_size = here["acq"], sizes["acq"]
    rows, length = echo_ref.shape[1:]
    lead = length // LANES
    pairs = turned.shape[0] // 2
    total = turned.shape[2]
    row_blocks = total // LANES
    half = PATCH // 2
    block = rows // echo_sem.shape[0]
    blocks = rows // block

    small = [
        pltpu.make_async_copy(src, dst, small_sem.at[n])
        for n, (src, dst) in enumerate(
            [(valid_hbm, valid_ref), (root_hbm, root_ref), (off_hbm, off_ref)]
        )
    ]
    consts = [
        pltpu.make_async_copy(src, dst, const_sem.at[n])
        for n, (src, dst) in enumerate([
            (af_hbm, af_ref), (ai_hbm, ai_ref), (fr_hbm, fr_ref), (ir_hbm, ir_ref),
            (fl_hbm, fl_ref), (il_hbm, il_ref),
        ])
    ]

    def load(b):
        at = pl.ds(pl.multiple_of(b * block, block), block)
        return pltpu.make_async_copy(
            echo_hbm.at[0, :, at, :], echo_ref.at[:, at, :], echo_sem.at[b]
        )

    small[0].start()
    for b in range(blocks):
        load(b).start()
    for copy in small[1:] + consts:
        copy.start()

    def device(axis, index):
        return tuple(index if name == axis else here[name] for name in names)

    def remote(src, dst, send, recv, axis, index):
        return pltpu.make_async_remote_copy(
            src_ref=src, dst_ref=dst, send_sem=send, recv_sem=recv,
            device_id=device(axis, index), device_id_type=pl.DeviceIdType.MESH,
        )

    barrier = pltpu.get_barrier_semaphore()
    targets = [("lines", (me + d) % peers) for d in range(1, peers)]
    targets += [("acq", (spot + d) % stack_size) for d in (1, stack_size - 1)]
    for axis, index in targets:
        pl.semaphore_signal(
            barrier, inc=1, device_id=device(axis, index), device_id_type=pl.DeviceIdType.MESH
        )

    per = LANES // lead
    parts = []
    for q in range(2):
        v = jnp.concatenate(
            [filt_in[0, q : q + 1, LANES * r : LANES * r + LANES] for r in range(lead)], axis=0
        ).T
        parts.append(
            jnp.concatenate([v[lead * m : lead * m + lead] for m in range(per)], axis=1)
        )
    filt_ref[0] = parts[0] * ph_ref[0] - parts[1] * ph_ref[1]
    filt_ref[1] = parts[0] * ph_ref[1] + parts[1] * ph_ref[0]

    right, left_of = (me + 1) % peers, (me + peers - 1) % peers
    edges = [
        remote(
            ref.at[:, pl.ds(0, LANES)], edge.at[n], edge_send.at[n], edge_recv.at[n],
            "lines", left_of,
        )
        for n, ref in enumerate((slope_ref, centre_ref))
    ]

    ahead = max(0, LAG * (stack_size - 2) - row_blocks - 4)
    opening = pairs - 1
    near_last = row_blocks * (pairs - 1) >= row_blocks + 1 + ahead
    early = pairs - 1 if near_last else pairs
    head = min(early, HEAD)
    order = sorted(range(1, peers), key=lambda d: -min(d, peers - d))

    def exchange(d, wave, first, count, r0, size):
        to = (me + d) % peers
        own = pl.ds(first, count)
        return remote(
            comp.at[to, own, :, pl.ds(r0, size), :],
            turned.at[own, :, pl.ds(pl.multiple_of(me * rows + r0, size), size), :],
            send_sem.at[0], recv_sem.at[wave], "lines", to,
        )

    def send_block(r0):
        for d in order:
            exchange(d, 0, 0, head, r0, block).start()

    def part_at(t):
        late = jnp.where(jnp.logical_and(t == early + 1, early < pairs), pairs - 1, t - 1)
        return jnp.where(t < early, t, jnp.where(t == early, 2 * pairs - 1, late))

    def send_part(t):
        p = part_at(t)
        for d in order:
            exchange(d, t - head + 1, p, 1, 0, rows).start()

    small[0].wait()

    def compress(b, carry):
        r0 = pl.multiple_of(b * block, block)
        load(b).wait()
        range_block(
            r0, block, me * rows, valid_ref[0], echo_ref, filt_ref, tw_ref, rf_ref, ri_ref,
            comp, zh, zl,
        )
        turned[:, :, pl.ds(pl.multiple_of(me * rows + r0, block), block), :] = comp[
            me, :, :, pl.ds(r0, block), :
        ]

        @pl.when(b == 0)
        def _():
            pl.semaphore_wait(barrier, len(targets))

        send_block(r0)
        return carry

    lax.fori_loop(0, blocks, compress, 0)
    for copy in edges:
        copy.start()

    send_part(head)

    image[:, :, :half, :] = jnp.zeros((2 * pairs + 1, 2, half, LANES), f32)
    image[:, :, half + total :, :] = jnp.zeros((2 * pairs + 1, 2, half, LANES), f32)

    @pl.when(spot == 0)
    def _():
        from_up[...] = jnp.zeros_like(from_up)

    @pl.when(spot == stack_size - 1)
    def _():
        from_down[...] = jnp.zeros_like(from_down)

    for copy in small[1:] + consts:
        copy.wait()
    for copy in edges:
        copy.wait_recv()
    lane = lax.broadcasted_iota(jnp.int32, (1, LANES), 1)
    for n, ref in enumerate((slope_ref, centre_ref)):
        row = [
            pltpu.roll(ref[:, LANES * a : LANES * a + LANES], LANES - half, 1)
            for a in range(2 * pairs)
        ]
        row.append(pltpu.roll(edge[n], LANES - half, 1))
        row = [jnp.where(lane < LANES - half, row[a], row[a + 1]) for a in range(2 * pairs)]
        for m in range(pairs):
            even, odd = row[2 * m], row[2 * m + 1]
            par_ref[m, n] = jnp.where(lane < PATCH, even, pltpu.roll(odd, PATCH, 1))
            par_ref[pairs + m, n] = jnp.where(lane < PATCH, pltpu.roll(even, PATCH, 1), odd)

    mine = root_ref[0] == spot
    lanes = (
        (spot, from_up, pass_up, up_send, up_recv, 1),
        (stack_size - 1 - spot, from_down, pass_down, down_send, down_recv, -1),
    )

    def chain(at, src, buffer, sends, recvs, step):
        return remote(
            src.at[at], buffer.at[at], sends.at[at], recvs.at[at], "acq",
            (spot + step + stack_size) % stack_size,
        )

    def slot(s, carry):
        for depth, buffer, staged, sends, recvs, step in lanes:
            at = s - LAG * (depth - 1)

            @pl.when(jnp.logical_and(depth > 0, jnp.logical_and(at >= 0, at < pairs * row_blocks)))
            def _():
                copy = chain(at, staged, buffer, sends, recvs, step)
                copy.wait_recv()

                @pl.when(depth < stack_size - 1)
                def _():
                    staged[at] = jnp.where(mine, crop[at], buffer[at])
                    copy.start()

        return carry

    def receive(wave, count):
        got = turned.at[pl.ds(0, count), :, pl.ds(0, rows * (peers - 1)), :]
        remote(got, got, send_sem.at[0], recv_sem.at[wave], "lines", right).wait_recv()

    wide_lane = lax.broadcasted_iota(jnp.int32, (LANES, LANES), 1)
    low = wide_lane < PATCH
    halo = remote(halo_out, halo_in, halo_send.at[0], halo_recv.at[0], "lines", right)

    def near(m):
        def start(a, carry):
            at = m * row_blocks + a
            line = pl.ds(pl.multiple_of(a * LANES + PATCH, PATCH), PATCH)
            for q in range(2):
                crop[at, q] = image[m, q, line, :].astype(bf16)
            for depth, buffer, staged, sends, recvs, step in lanes:
                @pl.when(jnp.logical_and(depth == 0, stack_size > 1))
                def _():
                    chain(at, crop, buffer, sends, recvs, step).start()
            return carry

        lax.fori_loop(0, row_blocks, start, 0)

    def far():
        p = 2 * pairs - 1
        for q in range(2):
            for a in range(row_blocks // 2):
                at = slice(LANES * a, LANES * a + LANES)
                above = slice(LANES * a + half, LANES * a + half + LANES)
                below = slice(above.start + total // 2, above.stop + total // 2)
                halo_out[q, at, :] = jnp.where(
                    low, pltpu.roll(image[p, q, above, :], PATCH, 1), image[p, q, below, :]
                ).astype(bf16)
        halo.start()

        @pl.when(me == peers - 1)
        def _():
            for q in range(2):
                for a in range(row_blocks):
                    at = slice(LANES * a + half, LANES * a + half + LANES)
                    image[p, q, at, :] = jnp.where(
                        wide_lane < LANES - half, image[p, q, at, :], 0.0
                    )

    def take_halo():
        halo.wait_recv()
        outside = jnp.logical_and(wide_lane < LANES - half, me == 0)
        for q in range(2):
            for a in range(row_blocks // 2):
                value = halo_in[q, LANES * a : LANES * a + LANES, :].astype(f32)
                to = half + LANES * a
                image[2 * pairs, q, to : to + LANES, :] = jnp.where(
                    outside, 0.0, pltpu.roll(value, PATCH, 1)
                )
                to += total // 2
                image[2 * pairs, q, to : to + LANES, :] = jnp.where(outside, 0.0, value)

    patch_lane = lax.broadcasted_iota(jnp.int32, (PATCH, LANES), 1)

    def put(i, kind, pair):
        at = pl.ds(pl.multiple_of(PATCH * (kind * row_blocks + i), PATCH), PATCH)
        for q in range(2):
            stack[at, LANES * q : LANES * q + LANES] = pair[q].astype(bf16)
        re, im = pair
        power[pl.ds(kind * row_blocks + i, 1), :] = jnp.sum(re * re + im * im, axis=0, keepdims=True)

    def window(m, i):
        picked = []
        for s in range(2):
            across = off_ref[0, 1, i, 2 * m + s]
            down = pl.ds(LANES * i + PATCH + off_ref[0, 0, i, 2 * m + s], PATCH)
            back = across < 0
            turn = across + jnp.where(back, PATCH, 0)
            before = pairs + m if s else jnp.where(m == 0, 2 * pairs, pairs + m - 1)
            first = jnp.where(back, before, m)
            second = jnp.where(back, m, pairs + m)
            base = jnp.where(back, PATCH * (1 - s), PATCH * s)
            start = patch_lane - PATCH * s < PATCH - turn
            picked.append([
                jnp.where(
                    start,
                    pltpu.roll(
                        image[first, q, down, :], (2 * LANES + PATCH * s - base - turn) % LANES, 1
                    ),
                    pltpu.roll(image[second, q, down, :], (PATCH + LANES - turn) % LANES, 1),
                )
                for q in range(2)
            ])
        return [jnp.where(patch_lane < PATCH, picked[0][q], picked[1][q]) for q in range(2)]

    def left(m_ref, value):
        y = dot(m_ref[...], value.astype(bf16))
        return y[:LANES] + y[LANES:]

    def right_product(value, m_ref):
        return dot(value, m_ref[0]) + dot(value, m_ref[1])

    def give(m):
        to = pl.ds(pl.multiple_of(m * LANES, LANES), LANES)
        return pltpu.make_async_copy(
            surface.at[:, :, to], out_ref.at[0, :, :, to], give_sem.at[m]
        )

    def correlate(m):
        def one(i, carry):
            put(i, 1, window(m, i))
            at = m * row_blocks + i
            put(i, 0, [
                jnp.where(
                    mine, crop[at, q],
                    jnp.where(root_ref[0] < spot, from_up[at, q], from_down[at, q]),
                ).astype(f32)
                for q in range(2)
            ])
            return carry

        lax.fori_loop(0, row_blocks, one, 0)
        y = right_product(stack[...], fr_ref)
        z = left(fl_ref, jnp.concatenate([
            jnp.concatenate(
                [
                    y[PATCH * n : PATCH * n + PATCH, LANES * q : LANES * q + LANES]
                    for n in range(2 * row_blocks)
                ],
                axis=1,
            )
            for q in range(2)
        ], axis=0))
        z, zs = z[:, : LANES * row_blocks], z[:, LANES * row_blocks :]
        pr, pi, sr, si = z[:PATCH], z[PATCH:], zs[:PATCH], zs[PATCH:]
        x = left(il_ref, jnp.concatenate([pr * sr + pi * si, pi * sr - pr * si], axis=0))
        x = jnp.concatenate([
            jnp.concatenate(
                [
                    x[PATCH * q : PATCH * q + PATCH, LANES * n : LANES * n + LANES]
                    for n in range(row_blocks)
                ],
                axis=0,
            )
            for q in range(2)
        ], axis=1)
        y = right_product(x.astype(bf16), ir_ref)
        level = power[...] * (1.0 / PATCH**2)
        side = lane < PATCH
        means = jnp.where(
            side,
            jnp.sum(jnp.where(side, level, 0.0), axis=1, keepdims=True),
            jnp.sum(jnp.where(side, 0.0, level), axis=1, keepdims=True),
        )
        scale = lax.rsqrt(means + eps)
        factor = scale[:row_blocks] * scale[row_blocks:] * (1.0 / PATCH**3)
        to = pl.ds(pl.multiple_of(m * LANES, LANES), LANES)
        for i in range(row_blocks):
            for q in range(2):
                surface[q, PATCH * i : PATCH * i + PATCH, to] = (
                    y[PATCH * i : PATCH * i + PATCH, LANES * q : LANES * q + LANES]
                    * factor[i : i + 1, :]
                )
        give(m).start()

    def slots(t, first, count):
        @pl.when(t >= opening)
        def _():
            at = (row_blocks + 1) * (t - opening)
            start = jnp.where(jnp.logical_and(t == opening, first <= 0), 0, at + first + ahead)
            stop = jnp.where(jnp.logical_and(t == opening, first < 0), 0, at + first + count + ahead)
            lax.fori_loop(start, stop, slot, 0)

    def step(t, carry):
        slots(t, -1, 1)

        @pl.when(t < 2 * pairs)
        def _():
            p = part_at(t)

            @pl.when(t == 0)
            def _():
                receive(0, head)

            @pl.when(t >= head)
            def _():
                receive(t - head + 1, 1)

            @pl.when(jnp.logical_and(jnp.logical_or(t == 0, t >= head), t < 2 * pairs - 2))
            def _():
                send_part(jnp.where(t == 0, head + 1, t + 2))

            azimuth_block(p, turned, par_ref, af_ref, ai_ref, image)

            @pl.when(p < pairs)
            def _():
                near(p)

            @pl.when(t == early)
            def _():
                far()

        slots(t, 0, 2)

        @pl.when(t > pairs)
        def _():
            @pl.when(t == pairs + 1)
            def _():
                take_halo()

            correlate(t - pairs - 1)

        slots(t, 2, 2)
        return carry

    lax.fori_loop(0, 2 * pairs + 1, step, 0)

    for depth, buffer, staged, sends, recvs, step_by in lanes:

        @pl.when(depth < stack_size - 1)
        def _():
            lax.fori_loop(
                0, pairs * row_blocks,
                lambda n, x: (chain(n, staged, buffer, sends, recvs, step_by).wait_send(), x)[1], 0,
            )

    halo.wait_send()
    for copy in edges:
        copy.wait_send()

    lax.fori_loop(0, pairs, lambda m, x: (give(m).wait(), x)[1], 0)
    sent = comp.at[pl.ds(0, peers - 1)]
    remote(sent, sent, send_sem.at[0], recv_sem.at[0], "lines", right).wait_send()


def focus(names, sizes, valid, root, echo, filt, slope, centre, offsets):
    rows, length = echo.shape[2:]
    lead = length // LANES
    block = min(rows, 32)
    blocks = rows // block
    total, cols = rows * sizes["lines"], slope.shape[1]
    peers = sizes["lines"]
    wide = 2 * LANES
    pairs = cols // wide
    row_blocks = total // LANES
    half = PATCH // 2
    place = np.arange(LANES)
    per = LANES // lead
    freq = per * (place % lead) + place // lead
    rf = halves(right_form(dft(LANES, -1.0)[:, freq]))
    ri = halves(right_form(dft(LANES, 1.0)[freq, :]))
    angle = 2 * np.pi * np.outer(np.arange(lead), place) / length
    tw = np.stack([np.cos(angle), -np.sin(angle)]).astype(np.float32)
    whole = np.arange(lead)[:, None] + lead * freq[None, :]
    angle = 2 * np.pi * ((half * whole) % length) / length
    ph = (np.stack([np.cos(angle), np.sin(angle)]) / length).astype(np.float32)
    fwd, inv = [], []
    for c in range(row_blocks):
        phase = np.exp(-2j * np.pi * c * place / total)
        matrix = dft(LANES, -1.0) * phase[None, :]
        fwd.append(left_form(matrix))
        inv.append(left_form(matrix.conj().T))
    fwd, inv = stacked(np.stack(fwd)), stacked(np.stack(inv))
    two = np.eye(2)
    fr = halves(right_form(np.kron(two, dft(PATCH, -1.0))))
    ir = halves(right_form(np.kron(two, dft(PATCH, 1.0))))
    fl = stacked(left_form(dft(PATCH, -1.0)))
    il = stacked(left_form(dft(PATCH, 1.0)))
    hbm, vmem = pl.BlockSpec(memory_space=pl.ANY), pl.BlockSpec(memory_space=pltpu.VMEM)
    dma = pltpu.SemaphoreType.DMA
    chunk = pltpu.VMEM((pairs * row_blocks, 2, PATCH, LANES), bf16)
    consts = (fwd, inv, fr, ir, fl, il)
    return pl.pallas_call(
        functools.partial(focus_body, names, sizes),
        in_specs=[hbm] * 4 + [vmem] * 7 + [hbm] * 6,
        out_specs=hbm,
        out_shape=jax.ShapeDtypeStruct((1, 2, total // 2, cols // 2), f32),
        scratch_shapes=[
            pltpu.SMEM(valid.shape, jnp.int32),
            pltpu.SMEM(root.shape, jnp.int32),
            pltpu.SMEM(offsets.shape, jnp.int32),
            pltpu.VMEM((2, rows, length), bf16),
        ]
        + [pltpu.VMEM(c.shape, c.dtype) for c in consts]
        + [
            pltpu.VMEM((2, lead, LANES), f32),
            pltpu.VMEM((2 * pairs, 2, 1, LANES), f32),
            pltpu.VMEM((2, 1, LANES), f32),
            pltpu.VMEM((lead * block, wide), bf16),
            pltpu.VMEM((lead * block, wide), bf16),
            pltpu.VMEM((peers, 2 * pairs, 2, rows, LANES), bf16),
            pltpu.VMEM((2 * pairs, 2, total, LANES), bf16),
            pltpu.VMEM((2 * pairs + 1, 2, total + PATCH, LANES), f32),
            pltpu.VMEM((2, total // 2, LANES), bf16),
            pltpu.VMEM((2, total // 2, LANES), bf16),
        ]
        + [chunk] * 5
        + [
            pltpu.VMEM((2 * row_blocks * PATCH, wide), bf16),
            pltpu.VMEM((2 * row_blocks, LANES), f32),
            pltpu.VMEM((2, total // 2, cols // 2), f32),
            dma((pairs,)),
        ]
        + [dma((3,)), dma((blocks,)), dma((len(consts),))]
        + [dma((1,)), dma((2 * pairs,))]
        + [dma((2,))] * 2
        + [dma((1,))] * 2
        + [dma((pairs * row_blocks,))] * 4,
        compiler_params=pltpu.CompilerParams(
            collective_id=0, has_side_effects=True, vmem_limit_bytes=63 * 1024 * 1024
        ),
        name="focus",
    )(valid, root, offsets, echo, filt, slope, centre, tw, ph, rf, ri, *consts)


def on_device(names, sizes, echo, filt, slope, centre, valid, reference_index, offsets):
    return focus(names, sizes, valid, reference_index, echo, filt, slope, centre, offsets)


def solution(mesh):
    names = tuple(mesh.axis_names)
    sizes = {name: int(mesh.shape[name]) for name in names}
    return jax.shard_map(
        functools.partial(on_device, names, sizes),
        mesh=mesh,
        in_specs=(
            P(("stack", "acq"), None, "lines", None),
            P(("stack", "acq"), None, None),
            P(("stack", "acq"), "lines"),
            P(("stack", "acq"), "lines"),
            P(("stack", "acq")),
            P("stack"),
            P(("stack", "acq"), None, None, "lines"),
        ),
        out_specs=P(("stack", "acq"), None, None, "lines"),
        check_vma=False,
    )
```

```python
import functools
import math

import jax
import jax.numpy as jnp
import numpy as np
from jax import lax
from jax.experimental import pallas as pl
from jax.experimental.pallas import tpu as pltpu
from jax.sharding import PartitionSpec as P

PATCH = 64
LANES = 128
eps = 1e-06
bf16 = jnp.bfloat16
f32 = jnp.float32


def dft(size, sign):
    index = np.arange(size)
    angle = 2.0 * np.pi * (np.outer(index, index) % size) / size
    return np.cos(angle) + 1j * sign * np.sin(angle)


def right_form(matrix):
    return np.block([[matrix.real, matrix.imag], [-matrix.imag, matrix.real]])


def left_form(matrix):
    return np.block([[matrix.real, -matrix.imag], [matrix.imag, matrix.real]])


def halves(matrix):
    high = np.asarray(matrix, np.float32).astype(bf16)
    low = (np.asarray(matrix, np.float64) - high.astype(np.float64)).astype(bf16)
    return np.stack([high, low])


def split(value):
    high = value.astype(bf16)
    return high, (value - high.astype(f32)).astype(bf16)


def dot(a, b):
    return jnp.dot(a, b, preferred_element_type=f32)


def dot_nt(a, b):
    return lax.dot_general(a, b, (((1,), (1,)), ((), ())), preferred_element_type=f32)


def dot_tn(a, b):
    return lax.dot_general(a, b, (((0,), (0,)), ((), ())), preferred_element_type=f32)


def fft_list(values, sign):
    count = len(values)
    if count == 1:
        return values
    even = fft_list(values[0::2], sign)
    odd = fft_list(values[1::2], sign)
    out = [None] * count
    for k in range(count // 2):
        re, im = odd[k]
        if k == 0:
            pass
        elif 4 * k == count:
            re, im = (-im, re) if sign > 0 else (im, -re)
        elif 8 * k == count:
            r = math.sqrt(0.5)
            re, im = ((re - im) * r, (re + im) * r) if sign > 0 else ((re + im) * r, (im - re) * r)
        elif 8 * k == 3 * count:
            r = math.sqrt(0.5)
            re, im = ((re + im) * -r, (re - im) * r) if sign > 0 else ((im - re) * r, (re + im) * -r)
        else:
            c = math.cos(2 * math.pi * k / count)
            s = sign * math.sin(2 * math.pi * k / count)
            re, im = re * c - im * s, re * s + im * c
        out[k] = (even[k][0] + re, even[k][1] + im)
        out[k + count // 2] = (even[k][0] - re, even[k][1] - im)
    return out


def range_block(r0, block, first, valid, echo_ref, filt_ref, tw_ref, fwd_ref, inv_ref, out_ref, zh, zl):
    lead = echo_ref.shape[2] // LANES
    peers, pairs = out_ref.shape[0], out_ref.shape[1] // 2
    group = 16
    low = lax.broadcasted_iota(jnp.int32, (group, LANES), 1) < PATCH

    def put(row, count, re, im):
        zh[row : row + count, :LANES], zl[row : row + count, :LANES] = split(re)
        zh[row : row + count, LANES:], zl[row : row + count, LANES:] = split(im)

    def product(m_ref):
        h = zh[...]
        return dot(h, m_ref[0]) + dot(zl[...], m_ref[0]) + dot(h, m_ref[1])

    for g in range(block // group):
        at = pl.multiple_of(r0 + g * group, group)
        line = first + at + lax.broadcasted_iota(jnp.int32, (group, 1), 0)
        keep = (line < valid).astype(f32)
        values = [
            tuple(
                echo_ref[q, pl.ds(at, group), LANES * a : LANES * a + LANES].astype(f32) * keep
                for q in range(2)
            )
            for a in range(lead)
        ]
        for c, (re, im) in enumerate(fft_list(values, -1.0)):
            tr, ti = tw_ref[0, c : c + 1, :], tw_ref[1, c : c + 1, :]
            put(c * block + g * group, group, re * tr - im * ti, re * ti + im * tr)
    y = product(fwd_ref)
    for c in range(lead):
        part = y[c * block : c * block + block]
        re, im = part[:, :LANES], part[:, LANES:]
        hr, hi = filt_ref[0, c : c + 1, :], filt_ref[1, c : c + 1, :]
        put(c * block, block, re * hr - im * hi, re * hi + im * hr)
    y = product(inv_ref)
    for g in range(block // group):
        at = pl.multiple_of(r0 + g * group, group)
        values = []
        for c in range(lead):
            part = y[c * block + g * group : c * block + g * group + group]
            re, im = part[:, :LANES], part[:, LANES:]
            tr, ti = tw_ref[0, c : c + 1, :], tw_ref[1, c : c + 1, :]
            values.append((re * tr + im * ti, im * tr - re * ti))
        values = fft_list(values, 1.0)
        for t in range(lead // 2):
            for q in range(2):
                even, odd = values[2 * t][q], values[2 * t + 1][q]
                near = jnp.where(low, even, pltpu.roll(odd, PATCH, 1))
                far = jnp.where(low, pltpu.roll(even, PATCH, 1), odd)
                to, m = divmod(t, pairs)
                out_ref[to, m, q, pl.ds(at, group), :] = near.astype(bf16)
                out_ref[to, pairs + m, q, pl.ds(at, group), :] = far.astype(bf16)


def unit_polys():
    z = 0.125 - 0.125 * np.cos(np.pi * (np.arange(400) + 0.5) / 400)
    f = np.sqrt(z)
    cosine = np.polynomial.Polynomial.fit(z, np.cos(2 * np.pi * f), 7, domain=[0, 0.25]).convert()
    sine = np.polynomial.Polynomial.fit(z, np.sin(2 * np.pi * f) / f, 6, domain=[0, 0.25]).convert()
    return [float(v) for v in cosine.coef], [float(v) for v in sine.coef]


def cos_sin_turns(turns):
    cosine, sine = unit_polys()
    frac = turns - jnp.round(turns)
    z = frac * frac

    def horner(coef):
        value = jnp.full_like(z, coef[-1])
        for v in coef[-2::-1]:
            value = value * z + v
        return value

    return horner(cosine), horner(sine) * frac


def stacked(matrix):
    return np.concatenate(list(halves(matrix)), axis=-2)


def both_halves(m, value):
    count = m.shape[0] // 2
    y = dot(m, jnp.concatenate(split(value), axis=1))
    y = y[:count] + y[count:]
    return y[:, :LANES] + y[:, LANES:]


def azimuth_block(p, in_ref, par_ref, fwd_ref, inv_ref, out_ref):
    total = in_ref.shape[2]
    lead = total // LANES
    values = [
        tuple(in_ref[p, q, LANES * a : LANES * a + LANES, :].astype(f32) for q in range(2))
        for a in range(lead)
    ]
    values = fft_list(values, -1.0)
    sharp = par_ref[p, 0] * (total / 8.0)
    centre = par_ref[p, 1]
    back = []
    for c in range(lead):
        y = both_halves(fwd_ref[c], jnp.concatenate(values[c], axis=0))
        k = c + lead * lax.broadcasted_iota(jnp.int32, (LANES, 1), 0)
        u = jnp.where(k >= total // 2, k - total, k).astype(f32) * (1.0 / total)
        w = u - centre
        co, si = cos_sin_turns(sharp * w * w)
        re, im = y[:LANES], y[LANES:]
        y = both_halves(
            inv_ref[c], jnp.concatenate([re * co - im * si, re * si + im * co], axis=0)
        )
        back.append((y[:LANES], y[LANES:]))
    half = PATCH // 2
    for a, pair in enumerate(fft_list(back, 1.0)):
        for q in range(2):
            value = (pair[q] * (1.0 / total)).astype(bf16).astype(f32)
            out_ref[p, q, LANES * a + half : LANES * a + half + LANES, :] = value


LAG = 5
HEAD = 3


def focus_body(
    names, sizes, valid_hbm, root_hbm, off_hbm, echo_hbm, filt_in, slope_ref, centre_ref,
    tw_ref, ph_ref, rf_ref, ri_ref, af_hbm, ai_hbm, fr_hbm, ir_hbm, fl_hbm, il_hbm,
    out_ref, valid_ref, root_ref, off_ref, echo_ref, af_ref, ai_ref, fr_ref, ir_ref, fl_ref,
    il_ref, filt_ref, par_ref, edge, zh, zl, comp, turned, image,
    halo_out, halo_in, crop, pass_up, pass_down, from_up, from_down, stack, power, surface, give_sem, small_sem, echo_sem, const_sem, send_sem, recv_sem, edge_send, edge_recv,
    halo_send, halo_recv, up_send, up_recv, down_send, down_recv,
):
    here = {name: lax.axis_index(name) for name in names}
    me, peers = here["lines"], sizes["lines"]
    spot, stack_size = here["acq"], sizes["acq"]
    rows, length = echo_ref.shape[1:]
    lead = length // LANES
    pairs = turned.shape[0] // 2
    total = turned.shape[2]
    row_blocks = total // LANES
    half = PATCH // 2
    block = rows // echo_sem.shape[0]
    blocks = rows // block

    small = [
        pltpu.make_async_copy(src, dst, small_sem.at[n])
        for n, (src, dst) in enumerate(
            [(valid_hbm, valid_ref), (root_hbm, root_ref), (off_hbm, off_ref)]
        )
    ]
    consts = [
        pltpu.make_async_copy(src, dst, const_sem.at[n])
        for n, (src, dst) in enumerate([
            (af_hbm, af_ref), (ai_hbm, ai_ref), (fr_hbm, fr_ref), (ir_hbm, ir_ref),
            (fl_hbm, fl_ref), (il_hbm, il_ref),
        ])
    ]

    def load(b):
        at = pl.ds(pl.multiple_of(b * block, block), block)
        return pltpu.make_async_copy(
            echo_hbm.at[0, :, at, :], echo_ref.at[:, at, :], echo_sem.at[b]
        )

    small[0].start()
    for b in range(blocks):
        load(b).start()
    for copy in small[1:] + consts:
        copy.start()

    def device(axis, index):
        return tuple(index if name == axis else here[name] for name in names)

    def remote(src, dst, send, recv, axis, index):
        return pltpu.make_async_remote_copy(
            src_ref=src, dst_ref=dst, send_sem=send, recv_sem=recv,
            device_id=device(axis, index), device_id_type=pl.DeviceIdType.MESH,
        )

    barrier = pltpu.get_barrier_semaphore()
    targets = [("lines", (me + d) % peers) for d in range(1, peers)]
    targets += [("acq", (spot + d) % stack_size) for d in (1, stack_size - 1)]
    for axis, index in targets:
        pl.semaphore_signal(
            barrier, inc=1, device_id=device(axis, index), device_id_type=pl.DeviceIdType.MESH
        )

    per = LANES // lead
    parts = []
    for q in range(2):
        v = jnp.concatenate(
            [filt_in[0, q : q + 1, LANES * r : LANES * r + LANES] for r in range(lead)], axis=0
        ).T
        parts.append(
            jnp.concatenate([v[lead * m : lead * m + lead] for m in range(per)], axis=1)
        )
    filt_ref[0] = parts[0] * ph_ref[0] - parts[1] * ph_ref[1]
    filt_ref[1] = parts[0] * ph_ref[1] + parts[1] * ph_ref[0]

    right, left_of = (me + 1) % peers, (me + peers - 1) % peers
    edges = [
        remote(
            ref.at[:, pl.ds(0, LANES)], edge.at[n], edge_send.at[n], edge_recv.at[n],
            "lines", left_of,
        )
        for n, ref in enumerate((slope_ref, centre_ref))
    ]

    ahead = max(0, LAG * (stack_size - 2) - row_blocks - 4)
    opening = pairs - 1
    near_last = row_blocks * (pairs - 1) >= row_blocks + 1 + ahead
    early = pairs - 1 if near_last else pairs
    head = min(early, HEAD)
    order = sorted(range(1, peers), key=lambda d: -min(d, peers - d))

    def exchange(d, wave, first, count, r0, size):
        to = (me + d) % peers
        own = pl.ds(first, count)
        return remote(
            comp.at[to, own, :, pl.ds(r0, size), :],
            turned.at[own, :, pl.ds(pl.multiple_of(me * rows + r0, size), size), :],
            send_sem.at[0], recv_sem.at[wave], "lines", to,
        )

    def send_block(r0):
        for d in order:
            exchange(d, 0, 0, head, r0, block).start()

    def part_at(t):
        late = jnp.where(jnp.logical_and(t == early + 1, early < pairs), pairs - 1, t - 1)
        return jnp.where(t < early, t, jnp.where(t == early, 2 * pairs - 1, late))

    def send_part(t):
        p = part_at(t)
        for d in order:
            exchange(d, t - head + 1, p, 1, 0, rows).start()

    small[0].wait()

    def compress(b, carry):
        r0 = pl.multiple_of(b * block, block)
        load(b).wait()
        range_block(
            r0, block, me * rows, valid_ref[0], echo_ref, filt_ref, tw_ref, rf_ref, ri_ref,
            comp, zh, zl,
        )
        turned[:, :, pl.ds(pl.multiple_of(me * rows + r0, block), block), :] = comp[
            me, :, :, pl.ds(r0, block), :
        ]

        @pl.when(b == 0)
        def _():
            pl.semaphore_wait(barrier, len(targets))

        send_block(r0)
        return carry

    lax.fori_loop(0, blocks, compress, 0)
    for copy in edges:
        copy.start()

    send_part(head)

    image[:, :, :half, :] = jnp.zeros((2 * pairs + 1, 2, half, LANES), f32)
    image[:, :, half + total :, :] = jnp.zeros((2 * pairs + 1, 2, half, LANES), f32)

    @pl.when(spot == 0)
    def _():
        from_up[...] = jnp.zeros_like(from_up)

    @pl.when(spot == stack_size - 1)
    def _():
        from_down[...] = jnp.zeros_like(from_down)

    for copy in small[1:] + consts:
        copy.wait()
    for copy in edges:
        copy.wait_recv()
    lane = lax.broadcasted_iota(jnp.int32, (1, LANES), 1)
    for n, ref in enumerate((slope_ref, centre_ref)):
        row = [
            pltpu.roll(ref[:, LANES * a : LANES * a + LANES], LANES - half, 1)
            for a in range(2 * pairs)
        ]
        row.append(pltpu.roll(edge[n], LANES - half, 1))
        row = [jnp.where(lane < LANES - half, row[a], row[a + 1]) for a in range(2 * pairs)]
        for m in range(pairs):
            even, odd = row[2 * m], row[2 * m + 1]
            par_ref[m, n] = jnp.where(lane < PATCH, even, pltpu.roll(odd, PATCH, 1))
            par_ref[pairs + m, n] = jnp.where(lane < PATCH, pltpu.roll(even, PATCH, 1), odd)

    mine = root_ref[0] == spot
    lanes = (
        (spot, from_up, pass_up, up_send, up_recv, 1),
        (stack_size - 1 - spot, from_down, pass_down, down_send, down_recv, -1),
    )

    def chain(at, src, buffer, sends, recvs, step):
        return remote(
            src.at[at], buffer.at[at], sends.at[at], recvs.at[at], "acq",
            (spot + step + stack_size) % stack_size,
        )

    def slot(s, carry):
        for depth, buffer, staged, sends, recvs, step in lanes:
            at = s - LAG * (depth - 1)

            @pl.when(jnp.logical_and(depth > 0, jnp.logical_and(at >= 0, at < pairs * row_blocks)))
            def _():
                copy = chain(at, staged, buffer, sends, recvs, step)
                copy.wait_recv()

                @pl.when(depth < stack_size - 1)
                def _():
                    staged[at] = jnp.where(mine, crop[at], buffer[at])
                    copy.start()

        return carry

    def receive(wave, count):
        got = turned.at[pl.ds(0, count), :, pl.ds(0, rows * (peers - 1)), :]
        remote(got, got, send_sem.at[0], recv_sem.at[wave], "lines", right).wait_recv()

    wide_lane = lax.broadcasted_iota(jnp.int32, (LANES, LANES), 1)
    low = wide_lane < PATCH
    halo = remote(halo_out, halo_in, halo_send.at[0], halo_recv.at[0], "lines", right)

    def near(m):
        def start(a, carry):
            at = m * row_blocks + a
            line = pl.ds(pl.multiple_of(a * LANES + PATCH, PATCH), PATCH)
            for q in range(2):
                crop[at, q] = image[m, q, line, :].astype(bf16)
            for depth, buffer, staged, sends, recvs, step in lanes:
                @pl.when(jnp.logical_and(depth == 0, stack_size > 1))
                def _():
                    chain(at, crop, buffer, sends, recvs, step).start()
            return carry

        lax.fori_loop(0, row_blocks, start, 0)

    def far():
        p = 2 * pairs - 1
        for q in range(2):
            for a in range(row_blocks // 2):
                at = slice(LANES * a, LANES * a + LANES)
                above = slice(LANES * a + half, LANES * a + half + LANES)
                below = slice(above.start + total // 2, above.stop + total // 2)
                halo_out[q, at, :] = jnp.where(
                    low, pltpu.roll(image[p, q, above, :], PATCH, 1), image[p, q, below, :]
                ).astype(bf16)
        halo.start()

        @pl.when(me == peers - 1)
        def _():
            for q in range(2):
                for a in range(row_blocks):
                    at = slice(LANES * a + half, LANES * a + half + LANES)
                    image[p, q, at, :] = jnp.where(
                        wide_lane < LANES - half, image[p, q, at, :], 0.0
                    )

    def take_halo():
        halo.wait_recv()
        outside = jnp.logical_and(wide_lane < LANES - half, me == 0)
        for q in range(2):
            for a in range(row_blocks // 2):
                value = halo_in[q, LANES * a : LANES * a + LANES, :].astype(f32)
                to = half + LANES * a
                image[2 * pairs, q, to : to + LANES, :] = jnp.where(
                    outside, 0.0, pltpu.roll(value, PATCH, 1)
                )
                to += total // 2
                image[2 * pairs, q, to : to + LANES, :] = jnp.where(outside, 0.0, value)

    patch_lane = lax.broadcasted_iota(jnp.int32, (PATCH, LANES), 1)

    def put(i, kind, pair):
        at = pl.ds(pl.multiple_of(PATCH * (kind * row_blocks + i), PATCH), PATCH)
        for q in range(2):
            stack[at, LANES * q : LANES * q + LANES] = pair[q].astype(bf16)
        re, im = pair
        power[pl.ds(kind * row_blocks + i, 1), :] = jnp.sum(re * re + im * im, axis=0, keepdims=True)

    def window(m, i):
        picked = []
        for s in range(2):
            across = off_ref[0, 1, i, 2 * m + s]
            down = pl.ds(LANES * i + PATCH + off_ref[0, 0, i, 2 * m + s], PATCH)
            back = across < 0
            turn = across + jnp.where(back, PATCH, 0)
            before = pairs + m if s else jnp.where(m == 0, 2 * pairs, pairs + m - 1)
            first = jnp.where(back, before, m)
            second = jnp.where(back, m, pairs + m)
            base = jnp.where(back, PATCH * (1 - s), PATCH * s)
            start = patch_lane - PATCH * s < PATCH - turn
            picked.append([
                jnp.where(
                    start,
                    pltpu.roll(
                        image[first, q, down, :], (2 * LANES + PATCH * s - base - turn) % LANES, 1
                    ),
                    pltpu.roll(image[second, q, down, :], (PATCH + LANES - turn) % LANES, 1),
                )
                for q in range(2)
            ])
        return [jnp.where(patch_lane < PATCH, picked[0][q], picked[1][q]) for q in range(2)]

    def left(m_ref, value):
        y = dot(m_ref[...], value.astype(bf16))
        return y[:LANES] + y[LANES:]

    def right_product(value, m_ref):
        return dot(value, m_ref[0]) + dot(value, m_ref[1])

    def give(m):
        to = pl.ds(pl.multiple_of(m * LANES, LANES), LANES)
        return pltpu.make_async_copy(
            surface.at[:, :, to], out_ref.at[0, :, :, to], give_sem.at[m]
        )

    def correlate(m):
        def one(i, carry):
            put(i, 1, window(m, i))
            at = m * row_blocks + i
            put(i, 0, [
                jnp.where(
                    mine, crop[at, q],
                    jnp.where(root_ref[0] < spot, from_up[at, q], from_down[at, q]),
                ).astype(f32)
                for q in range(2)
            ])
            return carry

        lax.fori_loop(0, row_blocks, one, 0, unroll=True)
        y = right_product(stack[...], fr_ref)
        z = left(fl_ref, jnp.concatenate([
            jnp.concatenate(
                [
                    y[PATCH * n : PATCH * n + PATCH, LANES * q : LANES * q + LANES]
                    for n in range(2 * row_blocks)
                ],
                axis=1,
            )
            for q in range(2)
        ], axis=0))
        z, zs = z[:, : LANES * row_blocks], z[:, LANES * row_blocks :]
        pr, pi, sr, si = z[:PATCH], z[PATCH:], zs[:PATCH], zs[PATCH:]
        x = left(il_ref, jnp.concatenate([pr * sr + pi * si, pi * sr - pr * si], axis=0))
        x = jnp.concatenate([
            jnp.concatenate(
                [
                    x[PATCH * q : PATCH * q + PATCH, LANES * n : LANES * n + LANES]
                    for n in range(row_blocks)
                ],
                axis=0,
            )
            for q in range(2)
        ], axis=1)
        y = right_product(x.astype(bf16), ir_ref)
        level = power[...] * (1.0 / PATCH**2)
        side = lane < PATCH
        means = jnp.where(
            side,
            jnp.sum(jnp.where(side, level, 0.0), axis=1, keepdims=True),
            jnp.sum(jnp.where(side, 0.0, level), axis=1, keepdims=True),
        )
        scale = lax.rsqrt(means + eps)
        factor = scale[:row_blocks] * scale[row_blocks:] * (1.0 / PATCH**3)
        to = pl.ds(pl.multiple_of(m * LANES, LANES), LANES)
        for i in range(row_blocks):
            for q in range(2):
                surface[q, PATCH * i : PATCH * i + PATCH, to] = (
                    y[PATCH * i : PATCH * i + PATCH, LANES * q : LANES * q + LANES]
                    * factor[i : i + 1, :]
                )
        give(m).start()

    def slots(t, first, count):
        @pl.when(t >= opening)
        def _():
            at = (row_blocks + 1) * (t - opening)
            start = jnp.where(jnp.logical_and(t == opening, first <= 0), 0, at + first + ahead)
            stop = jnp.where(jnp.logical_and(t == opening, first < 0), 0, at + first + count + ahead)
            lax.fori_loop(start, stop, slot, 0)

    def step(t, carry):
        slots(t, -1, 1)

        @pl.when(t < 2 * pairs)
        def _():
            p = part_at(t)

            @pl.when(t == 0)
            def _():
                receive(0, head)

            @pl.when(t >= head)
            def _():
                receive(t - head + 1, 1)

            @pl.when(jnp.logical_and(jnp.logical_or(t == 0, t >= head), t < 2 * pairs - 2))
            def _():
                send_part(jnp.where(t == 0, head + 1, t + 2))

            azimuth_block(p, turned, par_ref, af_ref, ai_ref, image)

            @pl.when(p < pairs)
            def _():
                near(p)

            @pl.when(t == early)
            def _():
                far()

        slots(t, 0, 2)

        @pl.when(t > pairs)
        def _():
            @pl.when(t == pairs + 1)
            def _():
                take_halo()

            correlate(t - pairs - 1)

        slots(t, 2, 2)
        return carry

    lax.fori_loop(0, 2 * pairs + 1, step, 0)

    for depth, buffer, staged, sends, recvs, step_by in lanes:

        @pl.when(depth < stack_size - 1)
        def _():
            lax.fori_loop(
                0, pairs * row_blocks,
                lambda n, x: (chain(n, staged, buffer, sends, recvs, step_by).wait_send(), x)[1], 0,
            )

    halo.wait_send()
    for copy in edges:
        copy.wait_send()

    lax.fori_loop(0, pairs, lambda m, x: (give(m).wait(), x)[1], 0)
    sent = comp.at[pl.ds(0, peers - 1)]
    remote(sent, sent, send_sem.at[0], recv_sem.at[0], "lines", right).wait_send()


def focus(names, sizes, valid, root, echo, filt, slope, centre, offsets):
    rows, length = echo.shape[2:]
    lead = length // LANES
    block = min(rows, 32)
    blocks = rows // block
    total, cols = rows * sizes["lines"], slope.shape[1]
    peers = sizes["lines"]
    wide = 2 * LANES
    pairs = cols // wide
    row_blocks = total // LANES
    half = PATCH // 2
    place = np.arange(LANES)
    per = LANES // lead
    freq = per * (place % lead) + place // lead
    rf = halves(right_form(dft(LANES, -1.0)[:, freq]))
    ri = halves(right_form(dft(LANES, 1.0)[freq, :]))
    angle = 2 * np.pi * np.outer(np.arange(lead), place) / length
    tw = np.stack([np.cos(angle), -np.sin(angle)]).astype(np.float32)
    whole = np.arange(lead)[:, None] + lead * freq[None, :]
    angle = 2 * np.pi * ((half * whole) % length) / length
    ph = (np.stack([np.cos(angle), np.sin(angle)]) / length).astype(np.float32)
    fwd, inv = [], []
    for c in range(row_blocks):
        phase = np.exp(-2j * np.pi * c * place / total)
        matrix = dft(LANES, -1.0) * phase[None, :]
        fwd.append(left_form(matrix))
        inv.append(left_form(matrix.conj().T))
    fwd, inv = stacked(np.stack(fwd)), stacked(np.stack(inv))
    two = np.eye(2)
    fr = halves(right_form(np.kron(two, dft(PATCH, -1.0))))
    ir = halves(right_form(np.kron(two, dft(PATCH, 1.0))))
    fl = stacked(left_form(dft(PATCH, -1.0)))
    il = stacked(left_form(dft(PATCH, 1.0)))
    hbm, vmem = pl.BlockSpec(memory_space=pl.ANY), pl.BlockSpec(memory_space=pltpu.VMEM)
    dma = pltpu.SemaphoreType.DMA
    chunk = pltpu.VMEM((pairs * row_blocks, 2, PATCH, LANES), bf16)
    consts = (fwd, inv, fr, ir, fl, il)
    return pl.pallas_call(
        functools.partial(focus_body, names, sizes),
        in_specs=[hbm] * 4 + [vmem] * 7 + [hbm] * 6,
        out_specs=hbm,
        out_shape=jax.ShapeDtypeStruct((1, 2, total // 2, cols // 2), f32),
        scratch_shapes=[
            pltpu.SMEM(valid.shape, jnp.int32),
            pltpu.SMEM(root.shape, jnp.int32),
            pltpu.SMEM(offsets.shape, jnp.int32),
            pltpu.VMEM((2, rows, length), bf16),
        ]
        + [pltpu.VMEM(c.shape, c.dtype) for c in consts]
        + [
            pltpu.VMEM((2, lead, LANES), f32),
            pltpu.VMEM((2 * pairs, 2, 1, LANES), f32),
            pltpu.VMEM((2, 1, LANES), f32),
            pltpu.VMEM((lead * block, wide), bf16),
            pltpu.VMEM((lead * block, wide), bf16),
            pltpu.VMEM((peers, 2 * pairs, 2, rows, LANES), bf16),
            pltpu.VMEM((2 * pairs, 2, total, LANES), bf16),
            pltpu.VMEM((2 * pairs + 1, 2, total + PATCH, LANES), f32),
            pltpu.VMEM((2, total // 2, LANES), bf16),
            pltpu.VMEM((2, total // 2, LANES), bf16),
        ]
        + [chunk] * 5
        + [
            pltpu.VMEM((2 * row_blocks * PATCH, wide), bf16),
            pltpu.VMEM((2 * row_blocks, LANES), f32),
            pltpu.VMEM((2, total // 2, cols // 2), f32),
            dma((pairs,)),
        ]
        + [dma((3,)), dma((blocks,)), dma((len(consts),))]
        + [dma((1,)), dma((2 * pairs,))]
        + [dma((2,))] * 2
        + [dma((1,))] * 2
        + [dma((pairs * row_blocks,))] * 4,
        compiler_params=pltpu.CompilerParams(
            collective_id=0, has_side_effects=True, vmem_limit_bytes=63 * 1024 * 1024
        ),
        name="focus",
    )(valid, root, offsets, echo, filt, slope, centre, tw, ph, rf, ri, *consts)


def on_device(names, sizes, echo, filt, slope, centre, valid, reference_index, offsets):
    return focus(names, sizes, valid, reference_index, echo, filt, slope, centre, offsets)


def solution(mesh):
    names = tuple(mesh.axis_names)
    sizes = {name: int(mesh.shape[name]) for name in names}
    return jax.shard_map(
        functools.partial(on_device, names, sizes),
        mesh=mesh,
        in_specs=(
            P(("stack", "acq"), None, "lines", None),
            P(("stack", "acq"), None, None),
            P(("stack", "acq"), "lines"),
            P(("stack", "acq"), "lines"),
            P(("stack", "acq")),
            P("stack"),
            P(("stack", "acq"), None, None, "lines"),
        ),
        out_specs=P(("stack", "acq"), None, None, "lines"),
        check_vma=False,
    )
```
